32 devices in a mesh: section: 4 (over y, x), dom: 8 (over z, core).
Axes of the slice: x: 2, y: 2, z: 4, core: 2. Of those that a mesh axis runs over, the one named last changes fastest.
Arguments:
- stacked: bfloat16 [4, 1024, 1024], P('section', 'dom'), may hold values from -6 to 6
- edges: int32 [1024, 256], P('dom'), may hold values 0 or 1
- picks: int32 [16, 3], P('dom'), may hold values from 0 to 2
- self_w: bfloat16 [4, 1024, 1024], P('section'), may hold values from -0.1875 to 0.1875
- neigh_w: bfloat16 [4, 1024, 1024], P('section'), may hold values from -0.75 to 0.75
Outputs:
- embeddings: bfloat16 [4, 1024, 1024], P('section', 'dom')
The draws below stay inside these ranges and needn't reach their ends.
Inputs may be any that keep to these rules, and one draw needn't show every extreme that they name: `picks`: A value of 2 means that the destination block has no tile from that direction; smaller values name a slab of the peer partition.
All inputs are finite; a program needn't handle non-finite values. No bound on the sum of `edges` on one device may be relied on, other than what follows from the above.
Results may differ from the reference program's by a relative error of at most 0.006.
Values may be sent and summed in bfloat16 or wider, within the bound.
A program may use at most 64 MiB of HBM per device.

```python
import jax
import jax.numpy as jnp

D = 1024
BLOCK = 64
SLABS = 2
LAYERS = 4
NODES = 1024
N_DOM = 8


def place_ends(entries, rng, low, high):
    longest = entries.shape.index(max(entries.shape))
    spots = []
    for shift in (0, 1):
        where = [jax.random.randint(jax.random.fold_in(rng, axis), (), 0, length) for axis, length in enumerate(entries.shape)]
        where[longest] = (where[longest] + shift) % entries.shape[longest]
        spots.append(tuple(where))
    return entries.at[spots[0]].set(low).at[spots[1]].set(high)


def levels(stream_key, extent, cuts, smallest, top_value):
    level = 1.0
    for dim, blocks in cuts:
        heights = jax.random.uniform(jax.random.fold_in(jax.random.fold_in(stream_key, 6), dim), (blocks,), jnp.float32, smallest / len(cuts), top_value / len(cuts))
        level = level * jnp.repeat(jnp.exp(heights), extent[dim] // blocks).reshape((-1,) + (1,) * (len(extent) - 1 - dim))
    return level


def gaussian(rng, shape, width, most, pieces=(), held_as=jnp.bfloat16):
    entries = jax.random.normal(rng, shape, jnp.float32) * width
    if len(pieces) > 0:
        entries = levels(rng, shape, pieces, -0.22, 0.18) * entries
    return jnp.clip(entries, min=-most, max=most).astype(held_as)


def setup_inputs(seed: int = 0) -> dict:
    arg_keys = jax.random.split(jax.random.key(seed), 6)
    stacked = gaussian(arg_keys[0], (LAYERS, NODES, D), 1.0, 6.0, ((0, 4), (1, 8)))
    edges = place_ends((jax.random.randint(arg_keys[1], (NODES, 4 * BLOCK), 0, 16) < 1).astype(jnp.int32), jax.random.fold_in(arg_keys[1], 1), 0, 1)
    picks = place_ends(jax.random.randint(arg_keys[2], (NODES // BLOCK, 3), 0, SLABS + 1), jax.random.fold_in(arg_keys[2], 1), 0, SLABS).astype(jnp.int32)
    self_w = gaussian(arg_keys[3], (LAYERS, D, D), D ** -0.5, 0.1875, ((0, 4),))
    neigh_w = gaussian(arg_keys[4], (LAYERS, D, D), (D // 16) ** -0.5, 0.75, ((0, 4),))
    return {"stacked": stacked, "edges": edges, "picks": picks, "self_w": self_w, "neigh_w": neigh_w}


def reference(stacked, edges, picks, self_w, neigh_w):
    layer_count = stacked.shape[0]
    node_total = stacked.shape[1]
    feature_width = stacked.shape[2]
    partitions = N_DOM
    peer_offsets = (-1, 1, 2)
    tile_table = edges.reshape(partitions, SLABS, BLOCK, 4, BLOCK)
    pick_table = picks.reshape(partitions, SLABS, 3)
    live_tiles = (pick_table < SLABS).astype(jnp.float32)
    clamped = jnp.minimum(pick_table, SLABS - 1).astype(jnp.int32)
    partition_ids = jnp.arange(partitions).astype(jnp.int32)
    current = stacked[0].reshape(partitions, SLABS, BLOCK, feature_width)
    results = []
    for layer_index in range(layer_count):
        history = stacked[layer_index].reshape(partitions, SLABS, BLOCK, feature_width)
        produced = []
        for slab_now in range(SLABS):
            fresh_mask = (jnp.arange(SLABS) <= slab_now)[None, :, None, None]
            source = jnp.where(fresh_mask, current, history)
            own_rows = current[:, slab_now]
            tile_zero = tile_table[:, slab_now, :, 0, :].astype(jnp.float32)
            summed = jnp.einsum("pij,pjd->pid", tile_zero, own_rows.astype(jnp.float32))
            degree = 1.0 + jnp.sum(tile_zero, axis=-1)
            for position in range(3):
                peer_field = jnp.roll(source, -peer_offsets[position], axis=0)
                blocks = peer_field[partition_ids, clamped[:, slab_now, position]]
                tile_mask = tile_table[:, slab_now, :, position + 1, :].astype(jnp.float32)
                tile_mask = tile_mask * live_tiles[:, slab_now, position][:, None, None]
                summed = summed + jnp.einsum("pij,pjd->pid", tile_mask, blocks.astype(jnp.float32))
                degree = degree + jnp.sum(tile_mask, axis=-1)
            mean_rows = (summed / degree[..., None]).astype(jnp.bfloat16)
            hidden = jnp.dot(own_rows.reshape(-1, feature_width), self_w[layer_index], preferred_element_type=jnp.float32)
            hidden = hidden + jnp.dot(mean_rows.reshape(-1, feature_width), neigh_w[layer_index], preferred_element_type=jnp.float32)
            produced.append(jnp.maximum(hidden, 0.0).astype(jnp.bfloat16).reshape(partitions, BLOCK, feature_width))
        current = jnp.stack(produced, axis=1)
        results.append(current.reshape(node_total, feature_width))
    return jnp.stack(results)
```

```python
import functools

import jax
import jax.numpy as jnp
from jax import lax
from jax.experimental import pallas as pl
from jax.experimental.pallas import tpu as pltpu
from jax.sharding import PartitionSpec as P

PEER_OFFSETS = (-1, 1, 2)
MESH = pl.DeviceIdType.MESH
BELOW, NEXT, FAR = range(3)
QUARTERS, PIECES = 4, 4
VIA = (1, 2)


def plan(nch, slabs):
    return {(j, nch - 1): VIA[j % len(VIA)] for j in range(slabs)}


def kernel(
    ns, nd, slabs, nch,
    stacked, edges_hbm, picks, ws_hbm, wn_hbm, out,
    ws, wn, vs, vn, edges, src, alt, masks, pre, acc, stage, above, sums, below, histsum,
    wsem, insem, outsem, zsend, zrecv, asend, psend, xsend, xrecv, tsend, trecv,
    ssend, srecv, hsend, hrecv, osend, orecv, vsend, vrecv, vpass, bsend, brecv, dsend,
):
    tiles = len(PEER_OFFSETS) + 1
    block = edges.shape[1] // tiles
    width = stacked.shape[1]
    cw = width // nch
    near, distant = list(range(nch // 2)), list(range(nch // 2, nch))
    half = cw * len(near)
    everywhere = list(range(nch))
    detour = plan(nch, slabs)
    last = slabs - 1
    s = lax.axis_index("section")
    p = lax.axis_index("dom")
    odd = lax.rem(p, 2)
    partner = p + 1 - 2 * odd
    across = lax.rem(p - 1 + 2 * odd + nd, nd)
    ahead, behind = lax.rem(p + 2, nd), lax.rem(p + nd - 2, nd)
    quarter = lax.rem(p, QUARTERS)
    twin = jnp.where(quarter < 2, p + 2, p - 2)
    top, helper, under = ns - 1, ns - 2, ns - 3
    is_first, is_top, is_helper = s == 0, s == top, s == helper
    is_mid = (s > 0) & (s <= under)
    sends_up = s <= under

    def at(section, dom):
        return {"section": section, "dom": dom}

    def rows(c):
        return pl.ds(c * block, block)

    def cols(ch):
        return pl.ds(ch * cw, cw)

    def own(slot, ch):
        return src.at[slot, rows(0), cols(ch)]

    def made_slot(c):
        return slabs + c

    def top_hist(j):
        return 2 * slabs - 1 + j

    e_copy = pltpu.make_async_copy(edges_hbm, edges, wsem.at[2])
    w_self = pltpu.make_async_copy(ws_hbm, ws, wsem.at[0])
    w_neigh = pltpu.make_async_copy(wn_hbm, wn, wsem.at[1])

    def given(j, slot):
        return pltpu.make_async_copy(stacked.at[rows(j)], src.at[slot, rows(0)], insem.at[j])

    @pl.when(is_first)
    def _():
        for j in range(slabs):
            given(j, j).start()

    @pl.when(is_mid | is_helper)
    def _():
        for j in range(1, slabs):
            given(j, j).start()

    @pl.when(is_top)
    def _():
        for j in range(1, slabs):
            given(j, top_hist(j)).start()

    barrier = pltpu.get_barrier_semaphore()

    def greet(section, dom):
        pl.semaphore_signal(barrier, inc=1, device_id=at(section, dom), device_id_type=MESH)

    for dom in (ahead, behind, across, partner):
        greet(s, dom)

    @pl.when(is_first)
    def _():
        for v in VIA:
            for dom in (ahead, across):
                greet(v, dom)

    for v in VIA:
        @pl.when(s == v)
        def _():
            greet(0, p)

    @pl.when(is_mid & (s > 1))
    def _():
        greet(s - 1, p)

    @pl.when(is_helper)
    def _():
        greet(top, p)
        greet(under, p)

    @pl.when(is_top)
    def _():
        greet(under, p)
        for dom in (p, ahead, across):
            greet(helper, dom)

    e_copy.start()

    w_self.start()
    w_neigh.start()

    def remote(src_ref, dst_ref, send, recv, section, dom):
        return pltpu.make_async_remote_copy(
            src_ref=src_ref, dst_ref=dst_ref, send_sem=send, recv_sem=recv,
            device_id=at(section, dom), device_id_type=MESH,
        )

    def peer(src_ref, slot, ch, k, sems, section):
        dom = behind if k == FAR else across
        return remote(
            src_ref, src.at[slot, rows(k + 1), cols(ch)],
            sems.at[slot, ch, k], zrecv.at[slot, ch, k], section, dom,
        )

    def spread(src_ref, slot, ch, sems, section, act):
        act(peer(src_ref, slot, ch, FAR, sems, section))

        @pl.when(odd == 1)
        def _():
            act(peer(src_ref, slot, ch, BELOW, sems, section))

    def start(copy):
        copy.start()

    def sent(copy):
        copy.wait_send()

    def share(slot, ch):
        return remote(
            own(slot, ch), src.at[slot, pl.ds((odd + 1) * block, block), cols(ch)],
            psend.at[slot, ch, 0], zrecv.at[slot, ch, odd], s, partner,
        )

    def handed(slot, ch):
        return remote(
            src.at[slot, rows(FAR + 1), cols(ch)], src.at[slot, rows(NEXT + 1), cols(ch)],
            psend.at[slot, ch, 1], zrecv.at[slot, ch, NEXT], s, partner,
        )

    def exchange(slot, ch):
        spread(own(slot, ch), slot, ch, zsend, s, start)
        share(slot, ch).start()

    def left(slot, ch, crossing=True):
        if crossing:
            spread(own(slot, ch), slot, ch, zsend, s, sent)
        sent(share(slot, ch))

    def relayed(slot):
        @pl.when(odd == 0)
        def _():
            for ch in range(nch):
                sent(handed(slot, ch))

    def exchanged(slot, crossing=everywhere):
        for ch in range(nch):
            left(slot, ch, ch in crossing)
        relayed(slot)

    def arrived(slot, ch, k):
        ref = src.at[slot, rows(k + 1), cols(ch)]
        pltpu.make_async_copy(ref, ref, zrecv.at[slot, ch, k]).wait()

    def relay(slot, ch):
        arrived(slot, ch, FAR)

        @pl.when(odd == 0)
        def _():
            handed(slot, ch).start()

    def rest(slot, ch):
        arrived(slot, ch, BELOW)
        arrived(slot, ch, NEXT)

    def up(c, ch, way=0):
        return remote(
            stage.at[c, :, cols(ch)], own(0, ch) if c == 0 else above.at[c - 1, :, cols(ch)],
            xsend.at[way, c, ch], xrecv.at[c, ch], s + 1 + way, p,
        )

    def sum_up(c, ch, way=0):
        return remote(
            sums.at[c - 1, :, cols(ch)], below.at[c - 1, :, cols(ch)],
            ssend.at[way, c - 1, ch], srecv.at[c - 1, ch], s + 1 + way, p,
        )

    def upward(copy, c, ch, act):
        @pl.when(s == under)
        def _():
            act(copy(c, ch, 1))

        act(copy(c, ch))

    def made_up(c, ch):
        return remote(
            stage.at[c, :, cols(ch)], own(made_slot(c), ch), bsend.at[c, ch], brecv.at[c, ch], top, p,
        )

    def lend(j, ch):
        return remote(
            own(j, ch), alt.at[j, :, cols(ch)], tsend.at[j, ch], trecv.at[j, ch], detour[j, ch], p,
        )

    def hist_up(c):
        return remote(sums.at[c], histsum.at[c], hsend.at[c], hrecv.at[c], top, p)

    def hand_back(c):
        return remote(
            src.at[made_slot(c), rows(0), pl.ds(0, half)], out.at[rows(c), pl.ds(0, half)],
            osend.at[c], orecv.at[c], helper, p,
        )

    depth = width // QUARTERS
    bit = depth // PIECES
    pieces = [(m, h) for m in range(2) for h in range(PIECES)]

    def part(pair, m, owner, h):
        return pair[m].at[pl.ds(owner * depth + h * bit, bit), pl.ds(0, half)]

    def weight_up(m, h):
        return remote(
            part((ws_hbm, wn_hbm), m, quarter, h), part((vs, vn), m, quarter, h),
            vsend.at[m, h], vrecv.at[m, 0, h], top, p,
        )

    def weight_pass(m, h, how):
        dom = twin if how == 2 else partner
        ref = part((vs, vn), m, quarter if how < 3 else lax.rem(quarter + 2, QUARTERS), h)
        return remote(ref, ref, vpass.at[m, how - 1, h], vrecv.at[m, how, h], s, dom)

    def weight_wait(m, how, h):
        ref = part((vs, vn), m, 0, h)
        pltpu.make_async_copy(ref, ref, vrecv.at[m, how, h]).wait()

    @pl.when(is_first)
    def _():
        for j in range(slabs):
            given(j, j).wait()

    @pl.when(is_mid | is_helper)
    def _():
        for j in range(1, slabs):
            given(j, j).wait()

    @pl.when(is_top)
    def _():
        for j in range(1, slabs):
            given(j, top_hist(j)).wait()

    def one(flag, amount=1):
        return jnp.where(flag, amount, 0)

    greetings = 4 + one(is_first, len(VIA)) + one(is_mid) + one(s == under) + one(is_helper, 3) + one(is_top)
    for v in VIA:
        greetings = greetings + one(s == v, 2)
    pl.semaphore_wait(barrier, greetings)

    @pl.when(is_first)
    def _():
        for (j, ch) in detour:
            lend(j, ch).start()
        for ch in range(nch):
            for j in range(slabs):
                if (j, ch) not in detour:
                    spread(own(j, ch), j, ch, zsend, s, start)
                share(j, ch).start()

    @pl.when(is_helper)
    def _():
        for m, h in pieces:
            weight_up(m, h).start()

    for v in VIA:
        @pl.when(s == v)
        def _():
            mine = [unit for unit in detour if detour[unit] == v]
            for (j, ch) in mine:
                lend(j, ch).wait_recv()
                spread(alt.at[j, :, cols(ch)], j, ch, asend, 0, start)
            for (j, ch) in mine:
                spread(alt.at[j, :, cols(ch)], j, ch, asend, 0, sent)

    @pl.when(is_mid | is_helper)
    def _():
        for j in range(1, slabs):
            for ch in range(nch):
                exchange(j, ch)

    @pl.when(is_top)
    def _():
        for j in range(1, slabs):
            for ch in range(nch):
                exchange(top_hist(j), ch)

    e_copy.wait()
    tile = lax.broadcasted_iota(jnp.int32, (block, edges.shape[1]), 1) // block
    degree = []
    for c in range(slabs):
        entries = edges[rows(c), :].astype(jnp.float32)
        total = jnp.ones((block, 1), jnp.float32)
        for j in range(slabs):
            scale = jnp.full(entries.shape, 1.0 if c == j else 0.0, jnp.float32)
            for k in range(len(PEER_OFFSETS)):
                wanted = jnp.where(picks[c, k] == j, 1.0, 0.0)
                scale = jnp.where(tile == k + 1, wanted, scale)
            masked = entries * scale
            masks[c, j] = masked.astype(jnp.bfloat16)
            total = total + jnp.sum(masked, axis=1, keepdims=True)
        degree.append(total)

    def gather(c, j, slot, ch):
        return jnp.dot(masks[c, j], src[slot, :, cols(ch)], preferred_element_type=jnp.float32)

    def gathers(c, pairs, ch):
        total = None
        for j, slot in pairs:
            term = gather(c, j, slot, ch)
            total = term if total is None else total + term
        return jnp.zeros((block, cw), jnp.float32) if total is None else total

    def span(chunks):
        return pl.ds(chunks[0] * cw, len(chunks) * cw)

    def self_part(c, ref, weights, chunks=everywhere):
        acc[c, :, span(chunks)] = jnp.dot(
            ref[...], weights[:, span(chunks)], preferred_element_type=jnp.float32
        )

    def finish(c, ch, summed, weights, emit, at_end, chunks=everywhere):
        mean = (summed / degree[c]).astype(jnp.bfloat16)
        if not at_end:
            acc[c, :, span(chunks)] += jnp.dot(
                mean, weights[cols(ch), span(chunks)], preferred_element_type=jnp.float32
            )
            return
        for n in chunks:
            hidden = acc[c, :, cols(n)] + jnp.dot(
                mean, weights[cols(ch), cols(n)], preferred_element_type=jnp.float32
            )
            emit(c, n, jnp.maximum(hidden, 0.0).astype(jnp.bfloat16))

    def put(c, n):
        return pltpu.make_async_copy(
            stage.at[c, :, cols(n)], out.at[rows(c), cols(n)], outsem.at[c, n]
        )

    def emit_up(c, n, made):
        stage[c, :, cols(n)] = made
        if c > 0:
            src[c + last, rows(0), cols(n)] = made
            exchange(c + last, n)
        upward(up, c, n, start)
        put(c, n).start()

    def emit_inner(c, n, made):
        src[made_slot(c), rows(0), cols(n)] = made
        exchange(made_slot(c), n)
        if n == near[-1]:
            hand_back(c).start()

    def emit_across(c, n, made):
        stage[c, :, cols(n)] = made
        made_up(c, n).start()
        spread(stage.at[c, :, cols(n)], made_slot(c), n, dsend, top, start)
        put(c, n).start()

    def emit_out(c, n, made):
        stage[c, :, cols(n)] = made
        put(c, n).start()

    def send_sums(c):
        relay(c + last, 0)
        for ch in range(nch):
            if ch + 1 < nch:
                relay(c + last, ch + 1)
            rest(c + last, ch)
            total = gathers(c, [(j, j + last) for j in range(1, c + 1)], ch)
            sums[c - 1, :, cols(ch)] = total.astype(jnp.bfloat16)
            upward(sum_up, c, ch, start)

    @pl.when(is_first)
    def _():
        w_self.wait()
        for c in range(slabs):
            self_part(c, src.at[c, rows(0)], ws)
        w_neigh.wait()
        everything = [(j, j) for j in range(slabs)]
        for j in range(slabs):
            relay(j, 0)
        for ch in range(nch):
            if ch + 1 < nch:
                for j in range(slabs):
                    relay(j, ch + 1)
            for j in range(slabs):
                rest(j, ch)
            finish(0, ch, gathers(0, everything, ch), wn, emit_up, ch == nch - 1)
        for c in range(1, slabs):
            for ch in range(nch):
                finish(c, ch, gathers(c, everything, ch), wn, emit_up, ch == nch - 1)
            send_sums(c)

    def first_slab_up():
        for ch in range(nch):
            up(0, ch).wait_recv()
            exchange(0, ch)

    def layer_above(w_s, w_n, emit, after, chunks=everywhere):
        self_part(0, src.at[0, rows(0)], w_s, chunks)
        relay(0, 0)
        for ch in range(nch):
            if ch + 1 < nch:
                relay(0, ch + 1)
            rest(0, ch)
            finish(0, ch, pre[0, :, cols(ch)] + gather(0, 0, 0, ch), w_n, emit, ch == nch - 1, chunks)
        for c in range(1, slabs):
            for ch in range(nch):
                pre[c, :, cols(ch)] += gather(c, 0, 0, ch)
            for ch in range(nch):
                up(c, ch).wait_recv()
            self_part(c, above.at[c - 1], w_s, chunks)
            for ch in range(nch):
                sum_up(c, ch).wait_recv()
                finish(
                    c, ch, pre[c, :, cols(ch)] + below[c - 1, :, cols(ch)].astype(jnp.float32),
                    w_n, emit, ch == nch - 1, chunks,
                )
            after(c)

    def take_hist(slot):
        for j in range(1, slabs):
            for ch in range(nch):
                relay(slot(j), ch)
        for j in range(1, slabs):
            for ch in range(nch):
                rest(slot(j), ch)

    def hist_into(slot, keep):
        for c in range(slabs):
            for ch in range(nch):
                keep(c, ch, gathers(c, [(j, slot(j)) for j in range(c + 1, slabs)], ch))

    def keep_pre(c, ch, total):
        pre[c, :, cols(ch)] = total

    def keep_sum(c, ch, total):
        sums[c, :, cols(ch)] = total.astype(jnp.bfloat16)

    @pl.when(is_mid)
    def _():
        take_hist(lambda j: j)
        hist_into(lambda j: j, keep_pre)
        w_self.wait()
        w_neigh.wait()
        first_slab_up()
        layer_above(ws, wn, emit_up, send_sums)

    @pl.when(is_helper)
    def _():
        take_hist(lambda j: j)
        hist_into(lambda j: j, keep_sum)
        for c in range(last):
            hist_up(c).start()
        hist_into(lambda j: j, keep_pre)
        w_self.wait()
        w_neigh.wait()
        first_slab_up()
        layer_above(ws, wn, emit_across, lambda c: None, distant)

    @pl.when(is_top)
    def _():
        take_hist(top_hist)
        for i, (m, h) in enumerate(pieces):
            weight_wait(m, 0, h)
            weight_pass(m, h, 1).start()
            weight_pass(m, h, 2).start()
            if i >= 2:
                weight_wait(pieces[i - 2][0], 2, pieces[i - 2][1])
                weight_pass(*pieces[i - 2], 3).start()
        for m, h in pieces[-2:]:
            weight_wait(m, 2, h)
            weight_pass(m, h, 3).start()
        for j in range(1, slabs):
            exchanged(top_hist(j))
        for m, h in pieces:
            weight_wait(m, 1, h)
            weight_wait(m, 3, h)
        for m, h in pieces:
            for how in (1, 2, 3):
                sent(weight_pass(m, h, how))
        w_self.wait()
        w_neigh.wait()
        first_slab_up()
        for c in range(slabs):
            if c < last:
                hist_up(c).wait_recv()
                pre[c] = histsum[c].astype(jnp.float32)
            else:
                pre[c] = jnp.zeros((block, width), jnp.float32)
        layer_above(vs, vn, emit_inner, lambda c: None, near)
        exchanged(0)
        hist_into(top_hist, keep_pre)
        for c in range(slabs):
            for ch in distant:
                made_up(c, ch).wait_recv()
                share(made_slot(c), ch).start()
            self_part(c, src.at[made_slot(c), rows(0)], ws)
            for j in range(c):
                for ch in range(nch):
                    pre[c, :, cols(ch)] += gather(c, j, made_slot(j), ch)
            for ch in range(nch):
                left(made_slot(c), ch, ch in near)
            sent(hand_back(c))
            order = distant + near
            relay(made_slot(c), order[0])
            for i, ch in enumerate(order):
                if i + 1 < nch:
                    relay(made_slot(c), order[i + 1])
                rest(made_slot(c), ch)
                finish(c, ch, pre[c, :, cols(ch)] + gather(c, c, made_slot(c), ch), wn, emit_out, i == nch - 1)
            relayed(made_slot(c))

    @pl.when(jnp.logical_not(is_helper))
    def _():
        for c in range(slabs):
            for n in range(nch):
                put(c, n).wait()

    @pl.when(is_helper)
    def _():
        for c in range(slabs):
            for ch in distant:
                put(c, ch).wait()
                sent(made_up(c, ch))
                spread(stage.at[c, :, cols(ch)], made_slot(c), ch, dsend, top, sent)

    @pl.when(is_first)
    def _():
        for j in range(slabs):
            for ch in range(nch):
                if (j, ch) in detour:
                    sent(lend(j, ch))
            exchanged(j, [ch for ch in range(nch) if (j, ch) not in detour])

    @pl.when(is_mid | is_helper)
    def _():
        for j in range(1, slabs):
            exchanged(j)
        exchanged(0)

    @pl.when(sends_up)
    def _():
        for ch in range(nch):
            for c in range(slabs):
                upward(up, c, ch, sent)
            for c in range(1, slabs):
                upward(sum_up, c, ch, sent)
        for c in range(1, slabs):
            exchanged(c + last)

    @pl.when(is_helper)
    def _():
        for m, h in pieces:
            sent(weight_up(m, h))
        for c in range(last):
            sent(hist_up(c))
        for c in range(slabs):
            hand_back(c).wait_recv()


def per_device(ns, nd, stacked, edges, picks, self_w, neigh_w):
    _, node_rows, width = stacked.shape
    tiles = len(PEER_OFFSETS) + 1
    block = edges.shape[1] // tiles
    slabs = node_rows // block
    nch = max(1, width // 256)
    slots = 3 * slabs - 1
    others = max(1, slabs - 1)
    anywhere = pl.BlockSpec(memory_space=pl.ANY)
    bf16, f32 = jnp.bfloat16, jnp.float32
    sem = pltpu.SemaphoreType.DMA
    result = pl.pallas_call(
        functools.partial(kernel, ns, nd, slabs, nch),
        out_shape=jax.ShapeDtypeStruct((node_rows, width), bf16),
        in_specs=[anywhere, anywhere, pl.BlockSpec(memory_space=pltpu.SMEM), anywhere, anywhere],
        out_specs=anywhere,
        scratch_shapes=[
            pltpu.VMEM((width, width), bf16),
            pltpu.VMEM((width, width), bf16),
            pltpu.VMEM((width, width // nch * (nch // 2)), bf16),
            pltpu.VMEM((width, width // nch * (nch // 2)), bf16),
            pltpu.VMEM(edges.shape, jnp.int32),
            pltpu.VMEM((slots, tiles * block, width), bf16),
            pltpu.VMEM((slabs, block, width), bf16),
            pltpu.VMEM((slabs, slabs, block, tiles * block), bf16),
            pltpu.VMEM((slabs, block, width), f32),
            pltpu.VMEM((slabs, block, width), f32),
            pltpu.VMEM((slabs, block, width), bf16),
            pltpu.VMEM((others, block, width), bf16),
            pltpu.VMEM((slabs, block, width), bf16),
            pltpu.VMEM((others, block, width), bf16),
            pltpu.VMEM((others, block, width), bf16),
            sem((3,)),
            sem((slabs,)),
            sem((slabs, nch)),
            sem((slots, nch, tiles - 1)),
            sem((slots, nch, tiles - 1)),
            sem((slabs, nch, tiles - 1)),
            sem((slots, nch, 2)),
            sem((2, slabs, nch)),
            sem((slabs, nch)),
            sem((slabs, nch)),
            sem((slabs, nch)),
            sem((2, others, nch)),
            sem((others, nch)),
            sem((others,)),
            sem((others,)),
            sem((slabs,)),
            sem((slabs,)),
            sem((2, PIECES)),
            sem((2, QUARTERS, PIECES)),
            sem((2, QUARTERS - 1, PIECES)),
            sem((slabs, nch)),
            sem((slabs, nch)),
            sem((slots, nch, tiles - 1)),
        ],
        compiler_params=pltpu.CompilerParams(collective_id=0, has_side_effects=True),
    )(stacked[0], edges, picks, self_w[0], neigh_w[0])
    return result[None]


def solution(mesh):
    in_specs = (
        P("section", "dom", None),
        P("dom", None),
        P("dom", None),
        P("section", None, None),
        P("section", None, None),
    )
    out_specs = P("section", "dom", None)
    ns, nd = mesh.shape["section"], mesh.shape["dom"]
    return jax.shard_map(
        functools.partial(per_device, ns, nd),
        mesh=mesh, in_specs=in_specs, out_specs=out_specs, check_vma=False,
    )
```

```python
import functools

import jax
import jax.numpy as jnp
from jax import lax
from jax.experimental import pallas as pl
from jax.experimental.pallas import tpu as pltpu
from jax.sharding import PartitionSpec as P

PEER_OFFSETS = (-1, 1, 2)
MESH = pl.DeviceIdType.MESH
BELOW, NEXT, FAR = range(3)
LANES = 128
QUARTERS, PIECES = 4, 4
VIA = (1, 2)


def plan(width):
    units = width // LANES
    near = units * 5 // 8
    far = units - near
    sizes = [near * 2 // 5, near - near * 2 // 5, far - far // 3, far // 3]
    starts = [sum(sizes[:i]) for i in range(len(sizes))]
    return {
        "sizes": sizes,
        "starts": starts,
        "near": [0, 1],
        "distant": [2, 3],
        "detour": {(0, 2): VIA[0], (1, 2): VIA[1]},
        "given": [0, 1, 3, 2],
        "inner": [0, 2, 1, 3],
        "twice": {3},
        "early": 1,
        "twice_given": {2},
    }


def kernel(
    ns, nd, slabs,
    stacked, edges_hbm, picks, ws_hbm, wn_hbm, out,
    ws, wn, vs, vn, edges, src, alt, masks, pre, acc, stage, above, sums, below, histsum,
    wsem, insem, outsem, gone, zrecv, hrecv, xrecv, arecv, srecv, brecv, trecv, qrecv, orecv,
    vrecv, precv,
):
    tiles = len(PEER_OFFSETS) + 1
    block = edges.shape[1] // tiles
    width = stacked.shape[1]
    how = plan(width)
    sizes, starts, near, distant = (how[key] for key in ("sizes", "starts", "near", "distant"))
    detour = {unit: via for unit, via in how["detour"].items() if unit[0] < slabs}
    everywhere = list(range(len(sizes)))
    half = sum(sizes[ch] for ch in near) * LANES
    last = slabs - 1
    s = lax.axis_index("section")
    p = lax.axis_index("dom")
    odd = lax.rem(p, 2)
    is_odd, is_even = odd == 1, odd == 0
    partner = p + 1 - 2 * odd
    across = lax.rem(p - 1 + 2 * odd + nd, nd)
    ahead, behind = lax.rem(p + 2, nd), lax.rem(p + nd - 2, nd)
    quarter = lax.rem(p, QUARTERS)
    twin = jnp.where(quarter < 2, p + 2, p - 2)
    top, helper, under = ns - 1, ns - 2, ns - 3
    is_first, is_top, is_helper = s == 0, s == top, s == helper
    is_mid = (s > 0) & (s <= under)
    sends_up = s <= under

    def at(section, dom):
        return {"section": section, "dom": dom}

    def rows(c):
        return pl.ds(c * block, block)

    def cols(ch):
        return pl.ds(starts[ch] * LANES, sizes[ch] * LANES)

    def span(chunks):
        return pl.ds(starts[chunks[0]] * LANES, sum(sizes[ch] for ch in chunks) * LANES)

    def own(slot, ch):
        return src.at[slot, rows(0), cols(ch)]

    def made_slot(c):
        return slabs + c

    def hist_slot(j):
        return 2 * slabs - 1 + j

    e_copy = pltpu.make_async_copy(edges_hbm, edges, wsem.at[2])
    w_self = pltpu.make_async_copy(ws_hbm, ws, wsem.at[0])
    w_neigh = pltpu.make_async_copy(wn_hbm, wn, wsem.at[1])

    def given(j, slot):
        return pltpu.make_async_copy(stacked.at[rows(j)], src.at[slot, rows(0)], insem.at[j])

    @pl.when(is_first)
    def _():
        for j in range(slabs):
            given(j, j).start()

    @pl.when(s > 0)
    def _():
        for j in range(1, slabs):
            given(j, hist_slot(j)).start()

    barrier = pltpu.get_barrier_semaphore()

    def greet(section, dom):
        pl.semaphore_signal(barrier, inc=1, device_id=at(section, dom), device_id_type=MESH)

    for dom in (ahead, behind, across, partner):
        greet(s, dom)

    @pl.when(is_first)
    def _():
        for v in VIA:
            for dom in (ahead, across):
                greet(v, dom)

    for v in VIA:
        @pl.when(s == v)
        def _():
            greet(0, p)

    @pl.when(is_mid & (s > 1))
    def _():
        greet(s - 1, p)

    @pl.when(is_helper)
    def _():
        greet(top, p)
        greet(under, p)

    @pl.when(is_top)
    def _():
        greet(under, p)
        for dom in (p, ahead, across):
            greet(helper, dom)

    e_copy.start()
    w_self.start()
    w_neigh.start()

    def remote(src_ref, dst_ref, recv, section, dom, send=0):
        return pltpu.make_async_remote_copy(
            src_ref=src_ref, dst_ref=dst_ref, send_sem=gone.at[send], recv_sem=recv,
            device_id=at(section, dom), device_id_type=MESH,
        )

    def landed(ref, sem):
        pltpu.make_async_copy(ref, ref, sem).wait()

    def drain(units, send=0):
        if units:
            landed(ws.at[pl.ds(0, units * block * LANES // width)], gone.at[send])

    def start(copy):
        copy.start()

    def peer(src_ref, slot, ch, k, section, send):
        dom = behind if k == FAR else across
        return remote(
            src_ref, src.at[slot, rows(k + 1), cols(ch)],
            zrecv.at[slot, ch, 0 if k == FAR else 1], section, dom, send,
        )

    def spread(src_ref, slot, ch, section, twice, send=0):
        start(peer(src_ref, slot, ch, FAR, section, send))

        @pl.when(is_odd)
        def _():
            start(peer(src_ref, slot, ch, BELOW, section, send))

        if ch in twice:
            @pl.when(is_even)
            def _():
                start(peer(src_ref, slot, ch, NEXT, section, send))

    def share(slot, ch):
        start(remote(
            own(slot, ch), src.at[slot, pl.ds((odd + 1) * block, block), cols(ch)],
            zrecv.at[slot, ch, 1], s, partner,
        ))

    def exchange(slot, ch, twice):
        spread(own(slot, ch), slot, ch, s, twice)
        share(slot, ch)

    def relay(slot, ch, twice):
        ref = src.at[slot, rows(FAR + 1), cols(ch)]
        landed(ref, zrecv.at[slot, ch, 0])
        if ch not in twice:
            @pl.when(is_even)
            def _():
                start(remote(
                    ref, src.at[slot, rows(NEXT + 1), cols(ch)], zrecv.at[slot, ch, 1], s, partner,
                ))

    def rest(slot, ch):
        landed(src.at[slot, pl.ds(block, 2 * block), cols(ch)], zrecv.at[slot, ch, 1])

    def hist_send(j):
        slot = hist_slot(j)
        mine = src.at[slot, rows(0)]
        start(remote(mine, src.at[slot, rows(FAR + 1)], hrecv.at[j - 1, 0], s, behind))

        @pl.when(is_odd)
        def _():
            start(remote(mine, src.at[slot, rows(BELOW + 1)], hrecv.at[j - 1, 1], s, across))

        start(remote(
            mine, src.at[slot, pl.ds((odd + 1) * block, block)], hrecv.at[j - 1, 1], s, partner,
        ))

    def hist_take(j):
        slot = hist_slot(j)
        ref = src.at[slot, rows(FAR + 1)]
        landed(ref, hrecv.at[j - 1, 0])

        @pl.when(is_even)
        def _():
            start(remote(ref, src.at[slot, rows(NEXT + 1)], hrecv.at[j - 1, 1], s, partner))

        landed(src.at[slot, pl.ds(block, 2 * block)], hrecv.at[j - 1, 1])

    def upward(src_ref, dst_ref, recv):
        start(remote(src_ref, dst_ref, recv, s + 1, p))

        @pl.when(s == under)
        def _():
            start(remote(src_ref, dst_ref, recv, s + 2, p, 1))

    def up(c, ch):
        part = stage.at[rows(c), cols(ch)]
        if c == 0:
            upward(part, own(0, ch), xrecv.at[ch])
        else:
            upward(part, above.at[c - 1, :, cols(ch)], arecv.at[c - 1])

    def sum_up(c, ch):
        upward(sums.at[c - 1, :, cols(ch)], below.at[c - 1, :, cols(ch)], srecv.at[c - 1, ch])

    def hand_back(c):
        return remote(
            src.at[made_slot(c), rows(0), pl.ds(0, half)], out.at[rows(c), pl.ds(0, half)],
            orecv.at[c], helper, p,
        )

    depth = width // QUARTERS
    bit = depth // PIECES
    pieces = [(m, h) for m in range(2) for h in range(PIECES)]

    def part(pair, m, owner, h):
        return pair[m].at[pl.ds(owner * depth + h * bit, bit), pl.ds(0, half)]

    def weight_up(m, h):
        start(remote(
            part((ws_hbm, wn_hbm), m, quarter, h), part((vs, vn), m, quarter, h),
            vrecv.at[0, m, h], top, p, 1,
        ))

    def weight_pass(m, h, dom, sem, owner, send=1):
        ref = part((vs, vn), m, owner, h)
        start(remote(ref, ref, sem, s, dom, send))

    @pl.when(is_first)
    def _():
        for j in range(slabs):
            given(j, j).wait()

    @pl.when(s > 0)
    def _():
        for j in range(1, slabs):
            given(j, hist_slot(j)).wait()

    def one(flag, amount=1):
        return jnp.where(flag, amount, 0)

    greetings = 4 + one(is_first, len(VIA)) + one(is_mid) + one(s == under) + one(is_helper, 3) + one(is_top)
    for v in VIA:
        greetings = greetings + one(s == v, 2)
    pl.semaphore_wait(barrier, greetings)

    def twice_given(j):
        return [ch for ch in how["twice_given"] if (j, ch) in detour]

    @pl.when(is_first)
    def _():
        for (j, ch), v in detour.items():
            start(remote(own(j, ch), alt.at[j, :, cols(ch)], trecv.at[j, ch], v, p))
        for ch in everywhere:
            for j in range(slabs):
                if (j, ch) not in detour:
                    spread(own(j, ch), j, ch, s, twice_given(j))
                share(j, ch)

    @pl.when(is_helper)
    def _():
        for m, h in pieces:
            weight_up(m, h)

    for v in VIA:
        @pl.when(s == v)
        def _():
            for (j, ch), via in detour.items():
                if via == v:
                    ref = alt.at[j, :, cols(ch)]
                    landed(ref, trecv.at[j, ch])
                    spread(ref, j, ch, 0, twice_given(j), 2)
            count = [sum(sizes[ch] for (j, ch), via in detour.items() if via == v), 0]
            count[1] = sum(
                sizes[ch] for (j, ch), via in detour.items() if via == v and ch in twice_given(j)
            )

            @pl.when(is_odd)
            def _():
                drain(2 * count[0], 2)

            @pl.when(is_even)
            def _():
                drain(count[0] + count[1], 2)

    @pl.when(s > 0)
    def _():
        for j in range(1, slabs):
            hist_send(j)

    e_copy.wait()
    tile = lax.broadcasted_iota(jnp.int32, (block, edges.shape[1]), 1) // block
    degree = []
    for c in range(slabs):
        entries = edges[rows(c), :].astype(jnp.float32)
        total = jnp.ones((block, 1), jnp.float32)
        for j in range(slabs):
            scale = jnp.full(entries.shape, 1.0 if c == j else 0.0, jnp.float32)
            for k in range(len(PEER_OFFSETS)):
                wanted = jnp.where(picks[c, k] == j, 1.0, 0.0)
                scale = jnp.where(tile == k + 1, wanted, scale)
            masked = entries * scale
            masks[j, rows(c)] = masked.astype(jnp.bfloat16)
            total = total + jnp.sum(masked, axis=1, keepdims=True)
        degree.append(total)

    degrees = jnp.concatenate(degree, axis=0)

    def gather(j, slot, ch, dest=slice(None)):
        return jnp.dot(masks[j, dest], src[slot, :, cols(ch)], preferred_element_type=jnp.float32)

    def gathers(pairs, ch, dest=slice(None)):
        total = None
        for j, slot in pairs:
            term = gather(j, slot, ch, dest)
            total = term if total is None else total + term
        return total

    def own_rows(slots):
        return jnp.concatenate([src[slot, rows(0), :] for slot in slots], axis=0)

    def self_part(c, ref, weights, chunks=everywhere):
        acc[rows(c), span(chunks)] = jnp.dot(
            ref[...], weights[:, span(chunks)], preferred_element_type=jnp.float32
        )

    def finish_all(ch, summed, weights, emit, at_end):
        mean = (summed / degrees).astype(jnp.bfloat16)
        if not at_end:
            acc[...] += jnp.dot(mean, weights[cols(ch), :], preferred_element_type=jnp.float32)
            return
        for c in range(slabs):
            for n in everywhere:
                hidden = acc[rows(c), cols(n)] + jnp.dot(
                    mean[c * block:(c + 1) * block], weights[cols(ch), cols(n)],
                    preferred_element_type=jnp.float32,
                )
                emit(c, n, jnp.maximum(hidden, 0.0).astype(jnp.bfloat16))

    def finish(c, ch, summed, weights, emit, at_end, chunks=everywhere):
        mean = (summed / degree[c]).astype(jnp.bfloat16)
        if not at_end:
            acc[rows(c), span(chunks)] += jnp.dot(
                mean, weights[cols(ch), span(chunks)], preferred_element_type=jnp.float32
            )
            return
        for n in chunks:
            hidden = acc[rows(c), cols(n)] + jnp.dot(
                mean, weights[cols(ch), cols(n)], preferred_element_type=jnp.float32
            )
            emit(c, n, jnp.maximum(hidden, 0.0).astype(jnp.bfloat16))

    def put(c, n):
        start(pltpu.make_async_copy(stage.at[rows(c), cols(n)], out.at[rows(c), cols(n)], outsem.at[0]))

    def emit_up(c, n, made):
        stage[rows(c), cols(n)] = made
        if c > 0:
            src[c + last, rows(0), cols(n)] = made
            exchange(c + last, n, how["twice"])
        up(c, n)
        put(c, n)

    def emit_inner(c, n, made):
        src[made_slot(c), rows(0), cols(n)] = made
        exchange(made_slot(c), n, how["twice"])
        if n == near[-1]:
            start(hand_back(c))

    def emit_across(c, n, made):
        stage[rows(c), cols(n)] = made
        part = stage.at[rows(c), cols(n)]
        start(remote(part, own(made_slot(c), n), brecv.at[c, distant.index(n)], top, p))
        spread(part, made_slot(c), n, top, how["twice"])
        put(c, n)

    def emit_out(c, n, made):
        stage[rows(c), cols(n)] = made
        put(c, n)

    def in_turn(order, ready, use):
        ready(order[0])
        for i, ch in enumerate(order):
            if i + 1 < len(order):
                ready(order[i + 1])
            use(ch, i == len(order) - 1)

    def send_sums(c):
        def ready(ch):
            relay(c + last, ch, how["twice"])

        def use(ch, at_end):
            rest(c + last, ch)
            total = gathers([(j, j + last) for j in range(1, c + 1)], ch, rows(c))
            sums[c - 1, :, cols(ch)] = total.astype(jnp.bfloat16)
            sum_up(c, ch)

        in_turn(everywhere, ready, use)

    @pl.when(is_first)
    def _():
        w_self.wait()
        acc[...] = jnp.dot(own_rows(range(slabs)), ws[...], preferred_element_type=jnp.float32)
        w_neigh.wait()

        def ready(ch):
            for j in range(slabs):
                relay(j, ch, twice_given(j))

        def use(ch, at_end):
            for j in range(slabs):
                rest(j, ch)
            finish_all(ch, gathers([(j, j) for j in range(slabs)], ch), wn, emit_up, at_end)

        in_turn(how["given"], ready, use)
        for c in range(1, slabs):
            send_sums(c)

    def first_slab_up():
        for ch in everywhere:
            landed(own(0, ch), xrecv.at[ch])
            exchange(0, ch, how["twice"])

    def layer_above(w_s, w_n, emit, after, chunks=everywhere):
        first_slab_up()
        self_part(0, src.at[0, rows(0)], w_s, chunks)

        def ready(ch):
            relay(0, ch, how["twice"])

        def use(ch, at_end):
            if ch == everywhere[how["early"]]:
                for c in range(1, slabs):
                    landed(above.at[c - 1], arecv.at[c - 1])
                    self_part(c, above.at[c - 1], w_s, chunks)
            rest(0, ch)
            total = pre[:, cols(ch)] + gather(0, 0, ch)
            pre[:, cols(ch)] = total
            finish(0, ch, total[:block], w_n, emit, at_end, chunks)

        in_turn(everywhere, ready, use)
        for c in range(1, slabs):
            for ch in everywhere:
                landed(below.at[c - 1, :, cols(ch)], srecv.at[c - 1, ch])
                finish(
                    c, ch, pre[rows(c), cols(ch)] + below[c - 1, :, cols(ch)].astype(jnp.float32),
                    w_n, emit, ch == everywhere[-1], chunks,
                )
            after(c)

    def hist_sums():
        for c in range(last):
            pre[rows(c)] = jnp.dot(
                masks[c + 1, rows(c)], src[hist_slot(c + 1)], preferred_element_type=jnp.float32
            )
            for j in range(c + 2, slabs):
                pre[rows(c)] += jnp.dot(
                    masks[j, rows(c)], src[hist_slot(j)], preferred_element_type=jnp.float32
                )
        pre[rows(last)] = jnp.zeros((block, width), jnp.float32)

    @pl.when(is_mid)
    def _():
        for j in range(1, slabs):
            hist_take(j)
        hist_sums()
        w_self.wait()
        w_neigh.wait()
        layer_above(ws, wn, emit_up, send_sums)

    @pl.when(is_helper)
    def _():
        for j in range(1, slabs):
            hist_take(j)
        hist_sums()
        for c in range(last):
            sums[c] = pre[rows(c)].astype(jnp.bfloat16)
            start(remote(sums.at[c], histsum.at[c], qrecv.at[c], top, p))
        w_self.wait()
        w_neigh.wait()
        layer_above(ws, wn, emit_across, lambda c: None, distant)

    @pl.when(is_top)
    def _():
        for m, h in pieces:
            landed(part((vs, vn), m, 0, h), vrecv.at[0, m, h])
            weight_pass(m, h, partner, precv.at[0], quarter)
            weight_pass(m, h, twin, vrecv.at[1, m, h], quarter, 2)
        for j in range(1, slabs):
            hist_take(j)
        for m, h in pieces:
            landed(part((vs, vn), m, 0, h), vrecv.at[1, m, h])
            weight_pass(m, h, partner, precv.at[1], lax.rem(quarter + 2, QUARTERS))
        everything = 2 * depth * half // (block * LANES)
        for i in range(2):
            landed(vs.at[pl.ds(0, 2 * depth), pl.ds(0, half)], precv.at[i])
        drain(2 * everything, 1)
        drain(everything, 2)
        for c in range(slabs):
            if c < last:
                landed(histsum.at[c], qrecv.at[c])
                pre[rows(c)] = histsum[c].astype(jnp.float32)
            else:
                pre[rows(c)] = jnp.zeros((block, width), jnp.float32)
        w_self.wait()
        w_neigh.wait()
        layer_above(vs, vn, emit_inner, lambda c: None, near)
        hist_sums()
        slots = [made_slot(c) for c in range(slabs)]

        def given_up(c):
            for ch in distant:
                landed(own(slots[c], ch), brecv.at[c, distant.index(ch)])
                share(slots[c], ch)

        for c in range(last):
            given_up(c)
            for ch in how["inner"]:
                relay(slots[c], ch, how["twice"])
        given_up(last)
        acc[...] = jnp.dot(own_rows(slots), ws[...], preferred_element_type=jnp.float32)

        def ready(ch):
            relay(slots[last], ch, how["twice"])

        def use(ch, at_end):
            for c in range(slabs):
                rest(slots[c], ch)
            total = pre[:, cols(ch)]
            for c in range(slabs):
                term = gather(c, slots[c], ch, pl.ds(c * block, (slabs - c) * block))
                if c > 0:
                    term = jnp.concatenate([jnp.zeros((c * block, term.shape[1]), jnp.float32), term], axis=0)
                total = total + term
            finish_all(ch, total, wn, emit_out, at_end)

        in_turn(how["inner"], ready, use)

    full = sum(sizes)
    part_units = sum(sizes[ch] for ch in distant)
    relayed_units = sum(sizes[ch] for ch in distant if ch not in how["twice"])

    def by_parity(even, odd_units):
        @pl.when(is_even)
        def _():
            drain(even)

        @pl.when(is_odd)
        def _():
            drain(odd_units)

    @pl.when(jnp.logical_not(is_helper))
    def _():
        landed(stage, outsem.at[0])

    @pl.when(is_first)
    def _():
        detoured = sum(sizes[ch] for _, ch in detour)
        twice_units = sum(sizes[ch] for j, ch in detour if ch in twice_given(j))
        base = 3 * full * slabs + full * slabs + last * 4 * full
        by_parity(base - twice_units, base - detoured)

    @pl.when(is_mid)
    def _():
        drain(3 * full * slabs + full * slabs + last * 4 * full)

    @pl.when(s == under)
    def _():
        @pl.when(sends_up)
        def _():
            drain(full * slabs + last * full, 1)

    @pl.when(is_helper)
    def _():
        landed(stage.at[:, span(distant)], outsem.at[0])
        drain(2 * depth * half // (block * LANES), 1)
        twice_units = part_units - relayed_units
        base = 3 * full * slabs + last * full + 2 * part_units * slabs
        by_parity(base + twice_units * slabs, base + part_units * slabs)
        for c in range(slabs):
            hand_back(c).wait_recv()

    @pl.when(is_top)
    def _():
        near_units = full - part_units
        base = 3 * full * slabs + 4 * near_units * slabs + part_units * slabs
        by_parity(base + relayed_units * slabs, base)


def per_device(ns, nd, stacked, edges, picks, self_w, neigh_w):
    _, node_rows, width = stacked.shape
    tiles = len(PEER_OFFSETS) + 1
    block = edges.shape[1] // tiles
    slabs = node_rows // block
    slots = 3 * slabs - 1
    others = max(1, slabs - 1)
    how = plan(width)
    nch = len(how["sizes"])
    half = sum(how["sizes"][ch] for ch in how["near"]) * LANES
    anywhere = pl.BlockSpec(memory_space=pl.ANY)
    bf16, f32 = jnp.bfloat16, jnp.float32
    sem = pltpu.SemaphoreType.DMA
    result = pl.pallas_call(
        functools.partial(kernel, ns, nd, slabs),
        out_shape=jax.ShapeDtypeStruct((node_rows, width), bf16),
        in_specs=[anywhere, anywhere, pl.BlockSpec(memory_space=pltpu.SMEM), anywhere, anywhere],
        out_specs=anywhere,
        scratch_shapes=[
            pltpu.VMEM((width, width), bf16),
            pltpu.VMEM((width, width), bf16),
            pltpu.VMEM((width, half), bf16),
            pltpu.VMEM((width, half), bf16),
            pltpu.VMEM(edges.shape, jnp.int32),
            pltpu.VMEM((slots, tiles * block, width), bf16),
            pltpu.VMEM((slabs, block, width), bf16),
            pltpu.VMEM((slabs, slabs * block, tiles * block), bf16),
            pltpu.VMEM((slabs * block, width), f32),
            pltpu.VMEM((slabs * block, width), f32),
            pltpu.VMEM((slabs * block, width), bf16),
            pltpu.VMEM((others, block, width), bf16),
            pltpu.VMEM((slabs, block, width), bf16),
            pltpu.VMEM((others, block, width), bf16),
            pltpu.VMEM((others, block, width), bf16),
            sem((3,)),
            sem((slabs,)),
            sem((1,)),
            sem((3,)),
            sem((2 * slabs, nch, 2)),
            sem((others, 2)),
            sem((nch,)),
            sem((others,)),
            sem((others, nch)),
            sem((slabs, len(how["distant"]))),
            sem((slabs, nch)),
            sem((others,)),
            sem((slabs,)),
            sem((2, 2, PIECES)),
            sem((2,)),
        ],
        compiler_params=pltpu.CompilerParams(collective_id=0, has_side_effects=True),
    )(stacked[0], edges, picks, self_w[0], neigh_w[0])
    return result[None]


def solution(mesh):
    in_specs = (
        P("section", "dom", None),
        P("dom", None),
        P("dom", None),
        P("section", None, None),
        P("section", None, None),
    )
    out_specs = P("section", "dom", None)
    ns, nd = mesh.shape["section"], mesh.shape["dom"]
    return jax.shard_map(
        functools.partial(per_device, ns, nd),
        mesh=mesh, in_specs=in_specs, out_specs=out_specs, check_vma=False,
    )
```

```python
import functools

import jax
import jax.numpy as jnp
from jax import lax
from jax.experimental import pallas as pl
from jax.experimental.pallas import tpu as pltpu
from jax.sharding import PartitionSpec as P

PEER_OFFSETS = (-1, 1, 2)
MESH = pl.DeviceIdType.MESH
BELOW, NEXT, FAR = range(3)
LANES = 128
QUARTERS, PIECES = 4, 4
VIA = (1, 2)


def plan(width):
    units = width // LANES
    near = units * 5 // 8
    far = units - near
    sizes = [near * 2 // 5, near - near * 2 // 5, far - far // 3, far // 3]
    starts = [sum(sizes[:i]) for i in range(len(sizes))]
    return {
        "sizes": sizes,
        "starts": starts,
        "near": [0, 1],
        "distant": [2, 3],
        "detour": {(0, 2): VIA[0], (1, 2): VIA[1]},
        "given": [0, 1, 3, 2],
        "twice": {3},
        "early": 1,
        "twice_given": {2},
    }


def kernel(
    ns, nd, slabs,
    stacked, edges_hbm, picks, ws_hbm, wn_hbm, out,
    ws, wn, vs, vn, edges, src, alt, masks, pre, acc, stage, above, sums, below, histsum,
    wsem, insem, outsem, gone, zrecv, hrecv, xrecv, arecv, srecv, brecv, trecv, qrecv, orecv,
    vrecv, precv,
):
    tiles = len(PEER_OFFSETS) + 1
    block = edges.shape[1] // tiles
    width = stacked.shape[1]
    how = plan(width)
    sizes, starts, near, distant = (how[key] for key in ("sizes", "starts", "near", "distant"))
    detour = {unit: via for unit, via in how["detour"].items() if unit[0] < slabs}
    everywhere = list(range(len(sizes)))
    half = sum(sizes[ch] for ch in near) * LANES
    last = slabs - 1
    s = lax.axis_index("section")
    p = lax.axis_index("dom")
    odd = lax.rem(p, 2)
    is_odd, is_even = odd == 1, odd == 0
    partner = p + 1 - 2 * odd
    across = lax.rem(p - 1 + 2 * odd + nd, nd)
    ahead, behind = lax.rem(p + 2, nd), lax.rem(p + nd - 2, nd)
    quarter = lax.rem(p, QUARTERS)
    twin = jnp.where(quarter < 2, p + 2, p - 2)
    top, helper, under = ns - 1, ns - 2, ns - 3
    is_first, is_top, is_helper = s == 0, s == top, s == helper
    is_mid = (s > 0) & (s <= under)
    sends_up = s <= under

    def at(section, dom):
        return {"section": section, "dom": dom}

    def rows(c):
        return pl.ds(c * block, block)

    def cols(ch):
        return pl.ds(starts[ch] * LANES, sizes[ch] * LANES)

    def span(chunks):
        return pl.ds(starts[chunks[0]] * LANES, sum(sizes[ch] for ch in chunks) * LANES)

    def own(slot, ch):
        return src.at[slot, rows(0), cols(ch)]

    def made_slot(c):
        return slabs + c

    def hist_slot(j):
        return 2 * slabs - 1 + j

    e_copy = pltpu.make_async_copy(edges_hbm, edges, wsem.at[2])
    w_self = pltpu.make_async_copy(ws_hbm, ws, wsem.at[0])
    w_neigh = pltpu.make_async_copy(wn_hbm, wn, wsem.at[1])

    def given(j, slot):
        return pltpu.make_async_copy(stacked.at[rows(j)], src.at[slot, rows(0)], insem.at[j])

    @pl.when(is_first)
    def _():
        for j in range(slabs):
            given(j, j).start()

    @pl.when(s > 0)
    def _():
        for j in range(1, slabs):
            given(j, hist_slot(j)).start()

    barrier = pltpu.get_barrier_semaphore()

    def greet(section, dom):
        pl.semaphore_signal(barrier, inc=1, device_id=at(section, dom), device_id_type=MESH)

    for dom in (ahead, behind, across, partner):
        greet(s, dom)

    @pl.when(is_first)
    def _():
        for v in VIA:
            for dom in (ahead, across):
                greet(v, dom)

    for v in VIA:
        @pl.when(s == v)
        def _():
            greet(0, p)

    @pl.when(is_mid & (s > 1))
    def _():
        greet(s - 1, p)

    @pl.when(is_helper)
    def _():
        greet(top, p)
        greet(under, p)

    @pl.when(is_top)
    def _():
        greet(under, p)
        for dom in (p, ahead, across):
            greet(helper, dom)

    e_copy.start()
    w_self.start()
    w_neigh.start()

    def remote(src_ref, dst_ref, recv, section, dom, send=0):
        return pltpu.make_async_remote_copy(
            src_ref=src_ref, dst_ref=dst_ref, send_sem=gone.at[send], recv_sem=recv,
            device_id=at(section, dom), device_id_type=MESH,
        )

    def landed(ref, sem):
        pltpu.make_async_copy(ref, ref, sem).wait()

    def drain(units, send=0):
        if units:
            landed(ws.at[pl.ds(0, units * block * LANES // width)], gone.at[send])

    def start(copy):
        copy.start()

    def peer(src_ref, slot, ch, k, section, send):
        dom = behind if k == FAR else across
        return remote(
            src_ref, src.at[slot, rows(k + 1), cols(ch)],
            zrecv.at[slot, ch, 0 if k == FAR else 1], section, dom, send,
        )

    def spread(src_ref, slot, ch, section, twice, send=0):
        start(peer(src_ref, slot, ch, FAR, section, send))

        @pl.when(is_odd)
        def _():
            start(peer(src_ref, slot, ch, BELOW, section, send))

        if ch in twice:
            @pl.when(is_even)
            def _():
                start(peer(src_ref, slot, ch, NEXT, section, send))

    def share(slot, ch):
        start(remote(
            own(slot, ch), src.at[slot, pl.ds((odd + 1) * block, block), cols(ch)],
            zrecv.at[slot, ch, 1], s, partner,
        ))

    def exchange(slot, ch, twice):
        spread(own(slot, ch), slot, ch, s, twice)
        share(slot, ch)

    def relay(slot, ch, twice):
        ref = src.at[slot, rows(FAR + 1), cols(ch)]
        landed(ref, zrecv.at[slot, ch, 0])
        if ch not in twice:
            @pl.when(is_even)
            def _():
                start(remote(
                    ref, src.at[slot, rows(NEXT + 1), cols(ch)], zrecv.at[slot, ch, 1], s, partner,
                ))

    def rest(slot, ch):
        landed(src.at[slot, pl.ds(block, 2 * block), cols(ch)], zrecv.at[slot, ch, 1])

    def hist_send(j):
        slot = hist_slot(j)
        mine = src.at[slot, rows(0)]
        start(remote(mine, src.at[slot, rows(FAR + 1)], hrecv.at[j - 1, 0], s, behind))

        @pl.when(is_odd)
        def _():
            start(remote(mine, src.at[slot, rows(BELOW + 1)], hrecv.at[j - 1, 1], s, across))

        start(remote(
            mine, src.at[slot, pl.ds((odd + 1) * block, block)], hrecv.at[j - 1, 1], s, partner,
        ))

    def hist_take(j):
        slot = hist_slot(j)
        ref = src.at[slot, rows(FAR + 1)]
        landed(ref, hrecv.at[j - 1, 0])

        @pl.when(is_even)
        def _():
            start(remote(ref, src.at[slot, rows(NEXT + 1)], hrecv.at[j - 1, 1], s, partner))

        landed(src.at[slot, pl.ds(block, 2 * block)], hrecv.at[j - 1, 1])

    def upward(src_ref, dst_ref, recv):
        start(remote(src_ref, dst_ref, recv, s + 1, p))

        @pl.when(s == under)
        def _():
            start(remote(src_ref, dst_ref, recv, s + 2, p, 1))

    def up(c, ch):
        part = stage.at[rows(c), cols(ch)]
        if c == 0:
            upward(part, own(0, ch), xrecv.at[ch])
        else:
            upward(part, above.at[c - 1, :, cols(ch)], arecv.at[c - 1])

    def sum_up(c, ch):
        upward(sums.at[c - 1, :, cols(ch)], below.at[c - 1, :, cols(ch)], srecv.at[c - 1, ch])

    def hand_back(c):
        return remote(
            src.at[made_slot(c), rows(0), pl.ds(0, half)], out.at[rows(c), pl.ds(0, half)],
            orecv.at[c], helper, p,
        )

    depth = width // QUARTERS
    bit = depth // PIECES
    pieces = [(m, h) for m in range(2) for h in range(PIECES)]

    def part(pair, m, owner, h):
        return pair[m].at[pl.ds(owner * depth + h * bit, bit), pl.ds(0, half)]

    def weight_up(m, h):
        start(remote(
            part((ws_hbm, wn_hbm), m, quarter, h), part((vs, vn), m, quarter, h),
            vrecv.at[0, m, h], top, p, 1,
        ))

    def weight_pass(m, h, dom, sem, owner, send=1):
        ref = part((vs, vn), m, owner, h)
        start(remote(ref, ref, sem, s, dom, send))

    @pl.when(is_first)
    def _():
        for j in range(slabs):
            given(j, j).wait()

    @pl.when(s > 0)
    def _():
        for j in range(1, slabs):
            given(j, hist_slot(j)).wait()

    def one(flag, amount=1):
        return jnp.where(flag, amount, 0)

    greetings = 4 + one(is_first, len(VIA)) + one(is_mid) + one(s == under) + one(is_helper, 3) + one(is_top)
    for v in VIA:
        greetings = greetings + one(s == v, 2)
    pl.semaphore_wait(barrier, greetings)

    def twice_given(j):
        return [ch for ch in how["twice_given"] if (j, ch) in detour]

    @pl.when(is_first)
    def _():
        for (j, ch), v in detour.items():
            start(remote(own(j, ch), alt.at[j, :, cols(ch)], trecv.at[j, ch], v, p))
        for ch in everywhere:
            for j in range(slabs):
                if (j, ch) not in detour:
                    spread(own(j, ch), j, ch, s, twice_given(j))
                share(j, ch)

    @pl.when(is_helper)
    def _():
        for m, h in pieces:
            weight_up(m, h)

    for v in VIA:
        @pl.when(s == v)
        def _():
            for (j, ch), via in detour.items():
                if via == v:
                    ref = alt.at[j, :, cols(ch)]
                    landed(ref, trecv.at[j, ch])
                    spread(ref, j, ch, 0, twice_given(j), 2)

    @pl.when(s > 0)
    def _():
        for j in range(1, slabs):
            hist_send(j)

    e_copy.wait()
    tile = lax.broadcasted_iota(jnp.int32, (block, edges.shape[1]), 1) // block
    degree = []
    for c in range(slabs):
        entries = edges[rows(c), :].astype(jnp.float32)
        total = jnp.ones((block, 1), jnp.float32)
        for j in range(slabs):
            scale = jnp.full(entries.shape, 1.0 if c == j else 0.0, jnp.float32)
            for k in range(len(PEER_OFFSETS)):
                wanted = jnp.where(picks[c, k] == j, 1.0, 0.0)
                scale = jnp.where(tile == k + 1, wanted, scale)
            masked = entries * scale
            masks[j, rows(c)] = masked.astype(jnp.bfloat16)
            total = total + jnp.sum(masked, axis=1, keepdims=True)
        degree.append(total)

    degrees = jnp.concatenate(degree, axis=0)

    def gather(j, slot, ch, dest=slice(None)):
        return jnp.dot(masks[j, dest], src[slot, :, cols(ch)], preferred_element_type=jnp.float32)

    def gathers(pairs, ch, dest=slice(None)):
        total = None
        for j, slot in pairs:
            term = gather(j, slot, ch, dest)
            total = term if total is None else total + term
        return total

    def own_rows(slots):
        return jnp.concatenate([src[slot, rows(0), :] for slot in slots], axis=0)

    def self_part(c, ref, weights, chunks=everywhere):
        acc[rows(c), span(chunks)] = jnp.dot(
            ref[...], weights[:, span(chunks)], preferred_element_type=jnp.float32
        )

    def finish_all(ch, summed, weights, emit, at_end):
        mean = (summed / degrees).astype(jnp.bfloat16)
        if not at_end:
            acc[...] += jnp.dot(mean, weights[cols(ch), :], preferred_element_type=jnp.float32)
            return
        for c in range(slabs):
            for n in everywhere:
                hidden = acc[rows(c), cols(n)] + jnp.dot(
                    mean[c * block:(c + 1) * block], weights[cols(ch), cols(n)],
                    preferred_element_type=jnp.float32,
                )
                emit(c, n, jnp.maximum(hidden, 0.0).astype(jnp.bfloat16))

    def finish(c, ch, summed, weights, emit, at_end, chunks=everywhere):
        mean = (summed / degree[c]).astype(jnp.bfloat16)
        if not at_end:
            acc[rows(c), span(chunks)] += jnp.dot(
                mean, weights[cols(ch), span(chunks)], preferred_element_type=jnp.float32
            )
            return
        for n in chunks:
            hidden = acc[rows(c), cols(n)] + jnp.dot(
                mean, weights[cols(ch), cols(n)], preferred_element_type=jnp.float32
            )
            emit(c, n, jnp.maximum(hidden, 0.0).astype(jnp.bfloat16))

    def put(c, n):
        start(pltpu.make_async_copy(stage.at[rows(c), cols(n)], out.at[rows(c), cols(n)], outsem.at[0]))

    def emit_up(c, n, made):
        stage[rows(c), cols(n)] = made
        if c > 0:
            src[c + last, rows(0), cols(n)] = made
            exchange(c + last, n, how["twice"])
        up(c, n)
        put(c, n)

    def emit_inner(c, n, made):
        src[made_slot(c), rows(0), cols(n)] = made
        exchange(made_slot(c), n, how["twice"])
        if n == near[-1]:
            start(hand_back(c))

    def emit_across(c, n, made):
        stage[rows(c), cols(n)] = made
        part = stage.at[rows(c), cols(n)]
        start(remote(part, own(made_slot(c), n), brecv.at[c, distant.index(n)], top, p))
        spread(part, made_slot(c), n, top, how["twice"])
        put(c, n)

    def emit_out(c, n, made):
        stage[rows(c), cols(n)] = made
        put(c, n)

    def in_turn(order, ready, use):
        ready(order[0])
        for i, ch in enumerate(order):
            if i + 1 < len(order):
                ready(order[i + 1])
            use(ch, i == len(order) - 1)

    def send_sums(c):
        def ready(ch):
            relay(c + last, ch, how["twice"])

        def use(ch, at_end):
            rest(c + last, ch)
            total = gathers([(j, j + last) for j in range(1, c + 1)], ch, rows(c))
            sums[c - 1, :, cols(ch)] = total.astype(jnp.bfloat16)
            sum_up(c, ch)

        in_turn(everywhere, ready, use)

    @pl.when(is_first)
    def _():
        w_self.wait()
        acc[...] = jnp.dot(own_rows(range(slabs)), ws[...], preferred_element_type=jnp.float32)
        w_neigh.wait()

        def ready(ch):
            for j in range(slabs):
                relay(j, ch, twice_given(j))

        def use(ch, at_end):
            for j in range(slabs):
                rest(j, ch)
            finish_all(ch, gathers([(j, j) for j in range(slabs)], ch), wn, emit_up, at_end)

        in_turn(how["given"], ready, use)
        for c in range(1, slabs):
            send_sums(c)

    def first_slab_up():
        for ch in everywhere:
            landed(own(0, ch), xrecv.at[ch])
            exchange(0, ch, how["twice"])

    def layer_above(w_s, w_n, emit, after, chunks=everywhere, weights_in=lambda: None):
        first_slab_up()
        weights_in()
        self_part(0, src.at[0, rows(0)], w_s, chunks)

        def ready(ch):
            relay(0, ch, how["twice"])

        def use(ch, at_end):
            if ch == everywhere[how["early"]]:
                for c in range(1, slabs):
                    landed(above.at[c - 1], arecv.at[c - 1])
                    self_part(c, above.at[c - 1], w_s, chunks)
            rest(0, ch)
            total = pre[:, cols(ch)] + gather(0, 0, ch)
            pre[:, cols(ch)] = total
            finish(0, ch, total[:block], w_n, emit, at_end, chunks)

        in_turn(everywhere, ready, use)
        for c in range(1, slabs):
            for ch in everywhere:
                landed(below.at[c - 1, :, cols(ch)], srecv.at[c - 1, ch])
                finish(
                    c, ch, pre[rows(c), cols(ch)] + below[c - 1, :, cols(ch)].astype(jnp.float32),
                    w_n, emit, ch == everywhere[-1], chunks,
                )
            after(c)

    def hist_sums():
        for c in range(last):
            pre[rows(c)] = jnp.dot(
                masks[c + 1, rows(c)], src[hist_slot(c + 1)], preferred_element_type=jnp.float32
            )
            for j in range(c + 2, slabs):
                pre[rows(c)] += jnp.dot(
                    masks[j, rows(c)], src[hist_slot(j)], preferred_element_type=jnp.float32
                )
        pre[rows(last)] = jnp.zeros((block, width), jnp.float32)

    @pl.when(is_mid)
    def _():
        for j in range(1, slabs):
            hist_take(j)
        hist_sums()
        w_self.wait()
        w_neigh.wait()
        layer_above(ws, wn, emit_up, send_sums)

    @pl.when(is_helper)
    def _():
        for j in range(1, slabs):
            hist_take(j)
        hist_sums()
        for c in range(last):
            sums[c] = pre[rows(c)].astype(jnp.bfloat16)
            start(remote(sums.at[c], histsum.at[c], qrecv.at[c], top, p))
        w_self.wait()
        w_neigh.wait()
        layer_above(ws, wn, emit_across, lambda c: None, distant)

    @pl.when(is_top)
    def _():
        for m, h in pieces:
            landed(part((vs, vn), m, 0, h), vrecv.at[0, m, h])
            weight_pass(m, h, partner, precv.at[0], quarter)
            weight_pass(m, h, twin, vrecv.at[1, m, h], quarter, 2)
        for j in range(1, slabs):
            hist_take(j)
        for m, h in pieces:
            landed(part((vs, vn), m, 0, h), vrecv.at[1, m, h])
            weight_pass(m, h, partner, precv.at[1], lax.rem(quarter + 2, QUARTERS))
        everything = 2 * depth * half // (block * LANES)

        def weights_in():
            for i in range(2):
                landed(vs.at[pl.ds(0, 2 * depth), pl.ds(0, half)], precv.at[i])

        for c in range(slabs):
            if c < last:
                landed(histsum.at[c], qrecv.at[c])
                pre[rows(c)] = histsum[c].astype(jnp.float32)
            else:
                pre[rows(c)] = jnp.zeros((block, width), jnp.float32)
        w_self.wait()
        w_neigh.wait()
        layer_above(vs, vn, emit_inner, lambda c: None, near, weights_in)
        drain(2 * everything, 1)
        drain(everything, 2)
        hist_sums()
        slots = [made_slot(c) for c in range(slabs)]

        def given_up(c):
            for ch in distant:
                landed(own(slots[c], ch), brecv.at[c, distant.index(ch)])
                share(slots[c], ch)

        def relays(c, chunks):
            for ch in chunks:
                relay(slots[c], ch, how["twice"])

        def use(ch, at_end=False):
            for c in range(slabs):
                rest(slots[c], ch)
            total = pre[:, cols(ch)]
            for c in range(slabs):
                term = gather(c, slots[c], ch, pl.ds(c * block, (slabs - c) * block))
                if c > 0:
                    term = jnp.concatenate([jnp.zeros((c * block, term.shape[1]), jnp.float32), term], axis=0)
                total = total + term
            finish_all(ch, total, wn, emit_out, at_end)

        def own_part(chunks):
            mine = jnp.concatenate([src[slot, rows(0), span(chunks)] for slot in slots], axis=0)
            return jnp.dot(mine, ws[span(chunks), :], preferred_element_type=jnp.float32)

        acc[...] = own_part(near)
        for c in range(slabs):
            relays(c, near)
        for c in range(slabs):
            given_up(c)
            relays(c, distant)
        acc[...] += own_part(distant)
        for ch in everywhere:
            use(ch, ch == everywhere[-1])

    full = sum(sizes)
    part_units = sum(sizes[ch] for ch in distant)
    relayed_units = sum(sizes[ch] for ch in distant if ch not in how["twice"])

    def by_parity(even, odd_units):
        @pl.when(is_even)
        def _():
            drain(even)

        @pl.when(is_odd)
        def _():
            drain(odd_units)

    @pl.when(jnp.logical_not(is_helper))
    def _():
        landed(stage, outsem.at[0])

    for v in VIA:
        @pl.when(s == v)
        def _():
            count = [sum(sizes[ch] for (j, ch), via in detour.items() if via == v), 0]
            count[1] = sum(
                sizes[ch] for (j, ch), via in detour.items() if via == v and ch in twice_given(j)
            )

            @pl.when(is_odd)
            def _():
                drain(2 * count[0], 2)

            @pl.when(is_even)
            def _():
                drain(count[0] + count[1], 2)

    @pl.when(is_first)
    def _():
        detoured = sum(sizes[ch] for _, ch in detour)
        twice_units = sum(sizes[ch] for j, ch in detour if ch in twice_given(j))
        base = 3 * full * slabs + full * slabs + last * 4 * full
        by_parity(base - twice_units, base - detoured)

    @pl.when(is_mid)
    def _():
        drain(3 * full * slabs + full * slabs + last * 4 * full)

    @pl.when(s == under)
    def _():
        @pl.when(sends_up)
        def _():
            drain(full * slabs + last * full, 1)

    @pl.when(is_helper)
    def _():
        landed(stage.at[:, span(distant)], outsem.at[0])
        drain(2 * depth * half // (block * LANES), 1)
        twice_units = part_units - relayed_units
        base = 3 * full * slabs + last * full + 2 * part_units * slabs
        by_parity(base + twice_units * slabs, base + part_units * slabs)
        for c in range(slabs):
            hand_back(c).wait_recv()

    @pl.when(is_top)
    def _():
        near_units = full - part_units
        base = 3 * full * slabs + 4 * near_units * slabs + part_units * slabs
        by_parity(base + relayed_units * slabs, base)


def per_device(ns, nd, stacked, edges, picks, self_w, neigh_w):
    _, node_rows, width = stacked.shape
    tiles = len(PEER_OFFSETS) + 1
    block = edges.shape[1] // tiles
    slabs = node_rows // block
    slots = 3 * slabs - 1
    others = max(1, slabs - 1)
    how = plan(width)
    nch = len(how["sizes"])
    half = sum(how["sizes"][ch] for ch in how["near"]) * LANES
    anywhere = pl.BlockSpec(memory_space=pl.ANY)
    bf16, f32 = jnp.bfloat16, jnp.float32
    sem = pltpu.SemaphoreType.DMA
    result = pl.pallas_call(
        functools.partial(kernel, ns, nd, slabs),
        out_shape=jax.ShapeDtypeStruct((node_rows, width), bf16),
        in_specs=[anywhere, anywhere, pl.BlockSpec(memory_space=pltpu.SMEM), anywhere, anywhere],
        out_specs=anywhere,
        scratch_shapes=[
            pltpu.VMEM((width, width), bf16),
            pltpu.VMEM((width, width), bf16),
            pltpu.VMEM((width, half), bf16),
            pltpu.VMEM((width, half), bf16),
            pltpu.VMEM(edges.shape, jnp.int32),
            pltpu.VMEM((slots, tiles * block, width), bf16),
            pltpu.VMEM((slabs, block, width), bf16),
            pltpu.VMEM((slabs, slabs * block, tiles * block), bf16),
            pltpu.VMEM((slabs * block, width), f32),
            pltpu.VMEM((slabs * block, width), f32),
            pltpu.VMEM((slabs * block, width), bf16),
            pltpu.VMEM((others, block, width), bf16),
            pltpu.VMEM((slabs, block, width), bf16),
            pltpu.VMEM((others, block, width), bf16),
            pltpu.VMEM((others, block, width), bf16),
            sem((3,)),
            sem((slabs,)),
            sem((1,)),
            sem((3,)),
            sem((2 * slabs, nch, 2)),
            sem((others, 2)),
            sem((nch,)),
            sem((others,)),
            sem((others, nch)),
            sem((slabs, len(how["distant"]))),
            sem((slabs, nch)),
            sem((others,)),
            sem((slabs,)),
            sem((2, 2, PIECES)),
            sem((2,)),
        ],
        compiler_params=pltpu.CompilerParams(collective_id=0, has_side_effects=True),
    )(stacked[0], edges, picks, self_w[0], neigh_w[0])
    return result[None]


def solution(mesh):
    in_specs = (
        P("section", "dom", None),
        P("dom", None),
        P("dom", None),
        P("section", None, None),
        P("section", None, None),
    )
    out_specs = P("section", "dom", None)
    ns, nd = mesh.shape["section"], mesh.shape["dom"]
    return jax.shard_map(
        functools.partial(per_device, ns, nd),
        mesh=mesh, in_specs=in_specs, out_specs=out_specs, check_vma=False,
    )
```

```python
import functools

import jax
import jax.numpy as jnp
from jax import lax
from jax.experimental import pallas as pl
from jax.experimental.pallas import tpu as pltpu
from jax.sharding import PartitionSpec as P

PEER_OFFSETS = (-1, 1, 2)
MESH = pl.DeviceIdType.MESH
BELOW, NEXT, FAR = range(3)
LANES = 128
QUARTERS, PIECES = 4, 4
VIA = (1, 2)


def plan(width):
    units = width // LANES
    near = units * 5 // 8
    far = units - near
    sizes = [near * 2 // 5, near - near * 2 // 5, far - far // 3, far // 3]
    starts = [sum(sizes[:i]) for i in range(len(sizes))]
    return {
        "sizes": sizes,
        "starts": starts,
        "near": [0, 1],
        "distant": [2, 3],
        "detour": {(0, 2): VIA[0], (1, 2): VIA[1]},
        "given": [0, 1, 3, 2],
        "twice": {3},
        "early": 1,
        "twice_given": {2},
    }


def kernel(
    ns, nd, slabs,
    stacked, edges_hbm, picks, ws_hbm, wn_hbm, out,
    ws, wn, vs, vn, edges, src, alt, masks, pre, acc, stage, above, sums, below, histsum,
    wsem, insem, outsem, gone, zrecv, hrecv, xrecv, arecv, srecv, brecv, trecv, qrecv, orecv,
    vrecv, precv,
):
    tiles = len(PEER_OFFSETS) + 1
    block = edges.shape[1] // tiles
    width = stacked.shape[1]
    how = plan(width)
    sizes, starts, near, distant = (how[key] for key in ("sizes", "starts", "near", "distant"))
    detour = {unit: via for unit, via in how["detour"].items() if unit[0] < slabs}
    everywhere = list(range(len(sizes)))
    half = sum(sizes[ch] for ch in near) * LANES
    last = slabs - 1
    s = lax.axis_index("section")
    p = lax.axis_index("dom")
    odd = lax.rem(p, 2)
    is_odd, is_even = odd == 1, odd == 0
    partner = p + 1 - 2 * odd
    across = lax.rem(p - 1 + 2 * odd + nd, nd)
    ahead, behind = lax.rem(p + 2, nd), lax.rem(p + nd - 2, nd)
    quarter = lax.rem(p, QUARTERS)
    twin = jnp.where(quarter < 2, p + 2, p - 2)
    top, helper, under = ns - 1, ns - 2, ns - 3
    is_first, is_top, is_helper = s == 0, s == top, s == helper
    is_mid = (s > 0) & (s <= under)
    sends_up = s <= under

    def at(section, dom):
        return {"section": section, "dom": dom}

    def rows(c):
        return pl.ds(c * block, block)

    def cols(ch):
        return pl.ds(starts[ch] * LANES, sizes[ch] * LANES)

    def span(chunks):
        return pl.ds(starts[chunks[0]] * LANES, sum(sizes[ch] for ch in chunks) * LANES)

    def own(slot, ch):
        return src.at[slot, rows(0), cols(ch)]

    def made_slot(c):
        return slabs + c

    def hist_slot(j):
        return 2 * slabs - 1 + j

    def lane(slot):
        return 1 if slot == 2 * slabs - 1 else slot

    e_copy = pltpu.make_async_copy(edges_hbm, edges, wsem.at[2])
    w_self = pltpu.make_async_copy(ws_hbm, ws, wsem.at[0])
    w_neigh = pltpu.make_async_copy(wn_hbm, wn, wsem.at[1])

    def given(j, slot):
        return pltpu.make_async_copy(stacked.at[rows(j)], src.at[slot, rows(0)], insem.at[j])

    @pl.when(is_first)
    def _():
        for j in range(slabs):
            given(j, j).start()

    @pl.when(s > 0)
    def _():
        for j in range(1, slabs):
            given(j, hist_slot(j)).start()

    barrier = pltpu.get_barrier_semaphore()

    def greet(section, dom):
        pl.semaphore_signal(barrier, inc=1, device_id=at(section, dom), device_id_type=MESH)

    for dom in (ahead, behind, across, partner):
        greet(s, dom)

    @pl.when(is_first)
    def _():
        for v in VIA:
            for dom in (ahead, across):
                greet(v, dom)

    for v in VIA:
        @pl.when(s == v)
        def _():
            greet(0, p)

    @pl.when(is_mid & (s > 1))
    def _():
        greet(s - 1, p)

    @pl.when(is_helper)
    def _():
        greet(top, p)
        greet(under, p)

    @pl.when(is_top)
    def _():
        greet(under, p)
        for dom in (p, ahead, across):
            greet(helper, dom)

    e_copy.start()
    w_self.start()
    w_neigh.start()

    def remote(src_ref, dst_ref, recv, section, dom, send=0):
        return pltpu.make_async_remote_copy(
            src_ref=src_ref, dst_ref=dst_ref, send_sem=gone.at[send], recv_sem=recv,
            device_id=at(section, dom), device_id_type=MESH,
        )

    def landed(ref, sem):
        pltpu.make_async_copy(ref, ref, sem).wait()

    def drain(units, send=0):
        if units:
            landed(ws.at[pl.ds(0, units * block * LANES // width)], gone.at[send])

    def start(copy):
        copy.start()

    def peer(src_ref, slot, ch, k, section, send):
        dom = behind if k == FAR else across
        return remote(
            src_ref, src.at[slot, rows(k + 1), cols(ch)],
            zrecv.at[lane(slot), ch, 0 if k == FAR else 1], section, dom, send,
        )

    def spread(src_ref, slot, ch, section, twice, send=0):
        start(peer(src_ref, slot, ch, FAR, section, send))

        @pl.when(is_odd)
        def _():
            start(peer(src_ref, slot, ch, BELOW, section, send))

        if ch in twice:
            @pl.when(is_even)
            def _():
                start(peer(src_ref, slot, ch, NEXT, section, send))

    def share(slot, ch):
        start(remote(
            own(slot, ch), src.at[slot, pl.ds((odd + 1) * block, block), cols(ch)],
            zrecv.at[lane(slot), ch, 1], s, partner,
        ))

    def exchange(slot, ch, twice):
        spread(own(slot, ch), slot, ch, s, twice)
        share(slot, ch)

    def relay(slot, ch, twice):
        ref = src.at[slot, rows(FAR + 1), cols(ch)]
        landed(ref, zrecv.at[lane(slot), ch, 0])
        if ch not in twice:
            @pl.when(is_even)
            def _():
                start(remote(
                    ref, src.at[slot, rows(NEXT + 1), cols(ch)], zrecv.at[lane(slot), ch, 1], s, partner,
                ))

    def rest(slot, ch):
        landed(src.at[slot, pl.ds(block, 2 * block), cols(ch)], zrecv.at[lane(slot), ch, 1])

    def hist_send(j):
        slot = hist_slot(j)
        mine = src.at[slot, rows(0)]
        start(remote(mine, src.at[slot, rows(FAR + 1)], hrecv.at[j - 1, 0], s, behind))

        @pl.when(is_odd)
        def _():
            start(remote(mine, src.at[slot, rows(BELOW + 1)], hrecv.at[j - 1, 1], s, across))

        start(remote(
            mine, src.at[slot, pl.ds((odd + 1) * block, block)], hrecv.at[j - 1, 1], s, partner,
        ))

    def hist_take(j):
        slot = hist_slot(j)
        ref = src.at[slot, rows(FAR + 1)]
        landed(ref, hrecv.at[j - 1, 0])

        @pl.when(is_even)
        def _():
            start(remote(ref, src.at[slot, rows(NEXT + 1)], hrecv.at[j - 1, 1], s, partner))

        landed(src.at[slot, pl.ds(block, 2 * block)], hrecv.at[j - 1, 1])

    def upward(src_ref, dst_ref, recv):
        start(remote(src_ref, dst_ref, recv, s + 1, p))

        @pl.when(s == under)
        def _():
            start(remote(src_ref, dst_ref, recv, s + 2, p, 1))

    def up(c, ch):
        part = stage.at[rows(c), cols(ch)]
        if c == 0:
            upward(part, own(0, ch), xrecv.at[ch])
        else:
            upward(part, above.at[c - 1, :, cols(ch)], arecv.at[c - 1])

    def sum_up(c, ch):
        upward(sums.at[c - 1, :, cols(ch)], below.at[c - 1, :, cols(ch)], srecv.at[c - 1, ch])

    def hand_back(c):
        return remote(
            src.at[made_slot(c), rows(0), pl.ds(0, half)], out.at[rows(c), pl.ds(0, half)],
            orecv.at[c], helper, p,
        )

    depth = width // QUARTERS
    bit = depth // PIECES
    pieces = [(m, h) for m in range(2) for h in range(PIECES)]

    def part(pair, m, owner, h):
        return pair[m].at[pl.ds(owner * depth + h * bit, bit), pl.ds(0, half)]

    def weight_up(m, h):
        start(remote(
            part((ws_hbm, wn_hbm), m, quarter, h), part((vs, vn), m, quarter, h),
            vrecv.at[0, m, h], top, p, 1,
        ))

    def weight_pass(m, h, dom, sem, owner, send=1):
        ref = part((vs, vn), m, owner, h)
        start(remote(ref, ref, sem, s, dom, send))

    @pl.when(is_first)
    def _():
        for j in range(slabs):
            given(j, j).wait()

    @pl.when(s > 0)
    def _():
        for j in range(1, slabs):
            given(j, hist_slot(j)).wait()

    def one(flag, amount=1):
        return jnp.where(flag, amount, 0)

    greetings = 4 + one(is_first, len(VIA)) + one(is_mid) + one(s == under) + one(is_helper, 3) + one(is_top)
    for v in VIA:
        greetings = greetings + one(s == v, 2)
    pl.semaphore_wait(barrier, greetings)

    def twice_given(j):
        return [ch for ch in how["twice_given"] if (j, ch) in detour]

    @pl.when(is_first)
    def _():
        for (j, ch), v in detour.items():
            start(remote(own(j, ch), alt.at[j, :, cols(ch)], trecv.at[j], v, p))
        for ch in everywhere:
            for j in range(slabs):
                if (j, ch) not in detour:
                    spread(own(j, ch), j, ch, s, twice_given(j))
                share(j, ch)

    @pl.when(is_helper)
    def _():
        for m, h in pieces:
            weight_up(m, h)

    for v in VIA:
        @pl.when(s == v)
        def _():
            for (j, ch), via in detour.items():
                if via == v:
                    ref = alt.at[j, :, cols(ch)]
                    landed(ref, trecv.at[j])
                    spread(ref, j, ch, 0, twice_given(j), 2)

    @pl.when(s > 0)
    def _():
        for j in range(1, slabs):
            hist_send(j)

    e_copy.wait()
    tile = lax.broadcasted_iota(jnp.int32, (block, edges.shape[1]), 1) // block
    degree = []
    for c in range(slabs):
        entries = edges[rows(c), :].astype(jnp.float32)
        total = jnp.ones((block, 1), jnp.float32)
        for j in range(slabs):
            scale = jnp.full(entries.shape, 1.0 if c == j else 0.0, jnp.float32)
            for k in range(len(PEER_OFFSETS)):
                wanted = jnp.where(picks[c, k] == j, 1.0, 0.0)
                scale = jnp.where(tile == k + 1, wanted, scale)
            masked = entries * scale
            masks[j, rows(c)] = masked.astype(jnp.bfloat16)
            total = total + jnp.sum(masked, axis=1, keepdims=True)
        degree.append(total)

    degrees = jnp.concatenate(degree, axis=0)

    def gather(j, slot, ch, dest=slice(None)):
        return jnp.dot(masks[j, dest], src[slot, :, cols(ch)], preferred_element_type=jnp.float32)

    def gathers(pairs, ch, dest=slice(None)):
        total = None
        for j, slot in pairs:
            term = gather(j, slot, ch, dest)
            total = term if total is None else total + term
        return total

    def own_rows(slots):
        return jnp.concatenate([src[slot, rows(0), :] for slot in slots], axis=0)

    def self_part(c, ref, weights, chunks=everywhere):
        acc[rows(c), span(chunks)] = jnp.dot(
            ref[...], weights[:, span(chunks)], preferred_element_type=jnp.float32
        )

    def finish_all(ch, summed, weights, emit, at_end):
        mean = (summed / degrees).astype(jnp.bfloat16)
        if not at_end:
            acc[...] += jnp.dot(mean, weights[cols(ch), :], preferred_element_type=jnp.float32)
            return
        for c in range(slabs):
            for n in everywhere:
                hidden = acc[rows(c), cols(n)] + jnp.dot(
                    mean[c * block:(c + 1) * block], weights[cols(ch), cols(n)],
                    preferred_element_type=jnp.float32,
                )
                emit(c, n, jnp.maximum(hidden, 0.0).astype(jnp.bfloat16))

    def finish(c, ch, summed, weights, emit, at_end, chunks=everywhere):
        mean = (summed / degree[c]).astype(jnp.bfloat16)
        if not at_end:
            acc[rows(c), span(chunks)] += jnp.dot(
                mean, weights[cols(ch), span(chunks)], preferred_element_type=jnp.float32
            )
            return
        for n in chunks:
            hidden = acc[rows(c), cols(n)] + jnp.dot(
                mean, weights[cols(ch), cols(n)], preferred_element_type=jnp.float32
            )
            emit(c, n, jnp.maximum(hidden, 0.0).astype(jnp.bfloat16))

    def put(c, chunks):
        start(pltpu.make_async_copy(
            stage.at[rows(c), span(chunks)], out.at[rows(c), span(chunks)], outsem.at[0]
        ))

    def emit_up(c, n, made):
        stage[rows(c), cols(n)] = made
        if c > 0:
            src[c + last, rows(0), cols(n)] = made
            exchange(c + last, n, how["twice"])
        up(c, n)
        if n == everywhere[-1]:
            put(c, everywhere)

    def emit_inner(c, n, made):
        src[made_slot(c), rows(0), cols(n)] = made
        exchange(made_slot(c), n, how["twice"])
        if n == near[-1]:
            start(hand_back(c))

    def emit_across(c, n, made):
        stage[rows(c), cols(n)] = made
        part = stage.at[rows(c), cols(n)]
        start(remote(part, own(made_slot(c), n), brecv.at[c, distant.index(n)], top, p))
        spread(part, made_slot(c), n, top, how["twice"])
        if n == distant[-1]:
            put(c, distant)

    def emit_out(c, n, made):
        stage[rows(c), cols(n)] = made
        put(c, [n])

    def in_turn(order, ready, use):
        ready(order[0])
        for i, ch in enumerate(order):
            if i + 1 < len(order):
                ready(order[i + 1])
            use(ch, i == len(order) - 1)

    def send_sums(c):
        def ready(ch):
            relay(c + last, ch, how["twice"])

        def use(ch, at_end):
            rest(c + last, ch)
            total = gathers([(j, j + last) for j in range(1, c + 1)], ch, rows(c))
            sums[c - 1, :, cols(ch)] = total.astype(jnp.bfloat16)
            sum_up(c, ch)

        in_turn(everywhere, ready, use)

    @pl.when(is_first)
    def _():
        w_self.wait()
        acc[...] = jnp.dot(own_rows(range(slabs)), ws[...], preferred_element_type=jnp.float32)
        w_neigh.wait()

        def ready(ch):
            for j in range(slabs):
                relay(j, ch, twice_given(j))

        def use(ch, at_end):
            for j in range(slabs):
                rest(j, ch)
            finish_all(ch, gathers([(j, j) for j in range(slabs)], ch), wn, emit_up, at_end)

        in_turn(how["given"], ready, use)
        for c in range(1, slabs):
            send_sums(c)

    def first_slab_up():
        for ch in everywhere:
            landed(own(0, ch), xrecv.at[ch])
            exchange(0, ch, how["twice"])

    def layer_above(w_s, w_n, emit, after, chunks=everywhere, weights_in=lambda: None):
        first_slab_up()
        weights_in()
        self_part(0, src.at[0, rows(0)], w_s, chunks)

        def ready(ch):
            relay(0, ch, how["twice"])

        def use(ch, at_end):
            if ch == everywhere[how["early"]]:
                for c in range(1, slabs):
                    landed(above.at[c - 1], arecv.at[c - 1])
                    self_part(c, above.at[c - 1], w_s, chunks)
            rest(0, ch)
            total = pre[:, cols(ch)] + gather(0, 0, ch)
            pre[:, cols(ch)] = total
            finish(0, ch, total[:block], w_n, emit, at_end, chunks)

        in_turn(everywhere, ready, use)
        for c in range(1, slabs):
            for ch in everywhere:
                landed(below.at[c - 1, :, cols(ch)], srecv.at[c - 1, ch])
                finish(
                    c, ch, pre[rows(c), cols(ch)] + below[c - 1, :, cols(ch)].astype(jnp.float32),
                    w_n, emit, ch == everywhere[-1], chunks,
                )
            after(c)

    def hist_sums():
        for c in range(last):
            pre[rows(c)] = jnp.dot(
                masks[c + 1, rows(c)], src[hist_slot(c + 1)], preferred_element_type=jnp.float32
            )
            for j in range(c + 2, slabs):
                pre[rows(c)] += jnp.dot(
                    masks[j, rows(c)], src[hist_slot(j)], preferred_element_type=jnp.float32
                )
        pre[rows(last)] = jnp.zeros((block, width), jnp.float32)

    @pl.when(is_mid)
    def _():
        for j in range(1, slabs):
            hist_take(j)
        hist_sums()
        w_self.wait()
        w_neigh.wait()
        layer_above(ws, wn, emit_up, send_sums)

    @pl.when(is_helper)
    def _():
        for j in range(1, slabs):
            hist_take(j)
        hist_sums()
        for c in range(last):
            sums[c] = pre[rows(c)].astype(jnp.bfloat16)
            start(remote(sums.at[c], histsum.at[c], qrecv.at[c], top, p))
        w_self.wait()
        w_neigh.wait()
        layer_above(ws, wn, emit_across, lambda c: None, distant)

    @pl.when(is_top)
    def _():
        for m, h in pieces:
            landed(part((vs, vn), m, 0, h), vrecv.at[0, m, h])
            weight_pass(m, h, partner, precv.at[0], quarter)
            weight_pass(m, h, twin, vrecv.at[1, m, h], quarter, 2)
        for j in range(1, slabs):
            hist_take(j)
        for m, h in pieces:
            landed(part((vs, vn), m, 0, h), vrecv.at[1, m, h])
            weight_pass(m, h, partner, precv.at[1], lax.rem(quarter + 2, QUARTERS))
        everything = 2 * depth * half // (block * LANES)

        def weights_in():
            for i in range(2):
                landed(vs.at[pl.ds(0, 2 * depth), pl.ds(0, half)], precv.at[i])

        for c in range(slabs):
            if c < last:
                landed(histsum.at[c], qrecv.at[c])
                pre[rows(c)] = histsum[c].astype(jnp.float32)
            else:
                pre[rows(c)] = jnp.zeros((block, width), jnp.float32)
        w_self.wait()
        w_neigh.wait()
        layer_above(vs, vn, emit_inner, lambda c: None, near, weights_in)
        drain(2 * everything, 1)
        drain(everything, 2)
        hist_sums()
        slots = [made_slot(c) for c in range(slabs)]

        def given_up(c):
            for ch in distant:
                landed(own(slots[c], ch), brecv.at[c, distant.index(ch)])
                share(slots[c], ch)

        def relays(c, chunks):
            for ch in chunks:
                relay(slots[c], ch, how["twice"])

        def use(ch, at_end=False):
            for c in range(slabs):
                rest(slots[c], ch)
            total = pre[:, cols(ch)]
            for c in range(slabs):
                term = gather(c, slots[c], ch, pl.ds(c * block, (slabs - c) * block))
                if c > 0:
                    term = jnp.concatenate([jnp.zeros((c * block, term.shape[1]), jnp.float32), term], axis=0)
                total = total + term
            finish_all(ch, total, wn, emit_out, at_end)

        def own_part(chunks):
            mine = jnp.concatenate([src[slot, rows(0), span(chunks)] for slot in slots], axis=0)
            return jnp.dot(mine, ws[span(chunks), :], preferred_element_type=jnp.float32)

        acc[...] = own_part(near)
        for c in range(slabs):
            relays(c, near)
        for c in range(slabs):
            given_up(c)
            relays(c, distant)
        acc[...] += own_part(distant)
        for ch in everywhere:
            use(ch, ch == everywhere[-1])

    full = sum(sizes)
    part_units = sum(sizes[ch] for ch in distant)
    relayed_units = sum(sizes[ch] for ch in distant if ch not in how["twice"])

    def by_parity(even, odd_units):
        @pl.when(is_even)
        def _():
            drain(even)

        @pl.when(is_odd)
        def _():
            drain(odd_units)

    @pl.when(jnp.logical_not(is_helper))
    def _():
        landed(stage, outsem.at[0])

    for v in VIA:
        @pl.when(s == v)
        def _():
            count = [sum(sizes[ch] for (j, ch), via in detour.items() if via == v), 0]
            count[1] = sum(
                sizes[ch] for (j, ch), via in detour.items() if via == v and ch in twice_given(j)
            )

            @pl.when(is_odd)
            def _():
                drain(2 * count[0], 2)

            @pl.when(is_even)
            def _():
                drain(count[0] + count[1], 2)

    @pl.when(is_first)
    def _():
        detoured = sum(sizes[ch] for _, ch in detour)
        twice_units = sum(sizes[ch] for j, ch in detour if ch in twice_given(j))
        base = 3 * full * slabs + full * slabs + last * 4 * full
        by_parity(base - twice_units, base - detoured)

    @pl.when(is_mid)
    def _():
        drain(3 * full * slabs + full * slabs + last * 4 * full)

    @pl.when(s == under)
    def _():
        @pl.when(sends_up)
        def _():
            drain(full * slabs + last * full, 1)

    @pl.when(is_helper)
    def _():
        landed(stage.at[:, span(distant)], outsem.at[0])
        drain(2 * depth * half // (block * LANES), 1)
        twice_units = part_units - relayed_units
        base = 3 * full * slabs + last * full + 2 * part_units * slabs
        by_parity(base + twice_units * slabs, base + part_units * slabs)
        for c in range(slabs):
            hand_back(c).wait_recv()

    @pl.when(is_top)
    def _():
        near_units = full - part_units
        base = 3 * full * slabs + 4 * near_units * slabs + part_units * slabs
        by_parity(base + relayed_units * slabs, base)


def per_device(ns, nd, stacked, edges, picks, self_w, neigh_w):
    _, node_rows, width = stacked.shape
    tiles = len(PEER_OFFSETS) + 1
    block = edges.shape[1] // tiles
    slabs = node_rows // block
    slots = 3 * slabs - 1
    others = max(1, slabs - 1)
    how = plan(width)
    nch = len(how["sizes"])
    half = sum(how["sizes"][ch] for ch in how["near"]) * LANES
    anywhere = pl.BlockSpec(memory_space=pl.ANY)
    bf16, f32 = jnp.bfloat16, jnp.float32
    sem = pltpu.SemaphoreType.DMA
    result = pl.pallas_call(
        functools.partial(kernel, ns, nd, slabs),
        out_shape=jax.ShapeDtypeStruct((node_rows, width), bf16),
        in_specs=[anywhere, anywhere, pl.BlockSpec(memory_space=pltpu.SMEM), anywhere, anywhere],
        out_specs=anywhere,
        scratch_shapes=[
            pltpu.VMEM((width, width), bf16),
            pltpu.VMEM((width, width), bf16),
            pltpu.VMEM((width, half), bf16),
            pltpu.VMEM((width, half), bf16),
            pltpu.VMEM(edges.shape, jnp.int32),
            pltpu.VMEM((slots, tiles * block, width), bf16),
            pltpu.VMEM((slabs, block, width), bf16),
            pltpu.VMEM((slabs, slabs * block, tiles * block), bf16),
            pltpu.VMEM((slabs * block, width), f32),
            pltpu.VMEM((slabs * block, width), f32),
            pltpu.VMEM((slabs * block, width), bf16),
            pltpu.VMEM((others, block, width), bf16),
            pltpu.VMEM((slabs, block, width), bf16),
            pltpu.VMEM((others, block, width), bf16),
            pltpu.VMEM((others, block, width), bf16),
            sem((3,)),
            sem((slabs,)),
            sem((1,)),
            sem((3,)),
            sem((max(2, 2 * slabs - 1), nch, 2)),
            sem((others, 2)),
            sem((nch,)),
            sem((others,)),
            sem((others, nch)),
            sem((slabs, len(how["distant"]))),
            sem((slabs,)),
            sem((others,)),
            sem((slabs,)),
            sem((2, 2, PIECES)),
            sem((2,)),
        ],
        compiler_params=pltpu.CompilerParams(collective_id=0, has_side_effects=True),
    )(stacked[0], edges, picks, self_w[0], neigh_w[0])
    return result[None]


def solution(mesh):
    in_specs = (
        P("section", "dom", None),
        P("dom", None),
        P("dom", None),
        P("section", None, None),
        P("section", None, None),
    )
    out_specs = P("section", "dom", None)
    ns, nd = mesh.shape["section"], mesh.shape["dom"]
    return jax.shard_map(
        functools.partial(per_device, ns, nd),
        mesh=mesh, in_specs=in_specs, out_specs=out_specs, check_vma=False,
    )
```

```python
import functools

import jax
import jax.numpy as jnp
from jax import lax
from jax.experimental import pallas as pl
from jax.experimental.pallas import tpu as pltpu
from jax.sharding import PartitionSpec as P

PEER_OFFSETS = (-1, 1, 2)
MESH = pl.DeviceIdType.MESH
BELOW, NEXT, FAR = range(3)
LANES = 128
QUARTERS, PIECES = 4, 2
VIA = (1, 2)


def plan(width):
    units = width // LANES
    near = units * 5 // 8
    far = units - near
    sizes = [near * 2 // 5, near - near * 2 // 5, far - far // 3, far // 3]
    starts = [sum(sizes[:i]) for i in range(len(sizes))]
    return {
        "sizes": sizes,
        "starts": starts,
        "near": [0, 1],
        "distant": [2, 3],
        "detour": {(0, 2): VIA[0], (1, 2): VIA[1]},
        "given": [0, 1, 3, 2],
        "twice": {3},
        "early": 1,
        "twice_given": {2},
    }


def kernel(
    ns, nd, slabs,
    stacked, edges_hbm, picks, ws_hbm, wn_hbm, out,
    ws, wn, vs, vn, edges, src, alt, masks, pre, acc, stage, above, sums, below, histsum,
    wsem, insem, outsem, gone, zrecv, hrecv, xrecv, arecv, srecv, brecv, trecv, qrecv, orecv,
    vrecv, precv,
):
    tiles = len(PEER_OFFSETS) + 1
    block = edges.shape[1] // tiles
    width = stacked.shape[1]
    how = plan(width)
    sizes, starts, near, distant = (how[key] for key in ("sizes", "starts", "near", "distant"))
    detour = {unit: via for unit, via in how["detour"].items() if unit[0] < slabs}
    everywhere = list(range(len(sizes)))
    half = sum(sizes[ch] for ch in near) * LANES
    last = slabs - 1
    s = lax.axis_index("section")
    p = lax.axis_index("dom")
    odd = lax.rem(p, 2)
    is_odd, is_even = odd == 1, odd == 0
    partner = p + 1 - 2 * odd
    across = lax.rem(p - 1 + 2 * odd + nd, nd)
    ahead, behind = lax.rem(p + 2, nd), lax.rem(p + nd - 2, nd)
    quarter = lax.rem(p, QUARTERS)
    twin = jnp.where(quarter < 2, p + 2, p - 2)
    top, helper, under = ns - 1, ns - 2, ns - 3
    is_first, is_top, is_helper = s == 0, s == top, s == helper
    is_mid = (s > 0) & (s <= under)
    sends_up = s <= under

    def at(section, dom):
        return {"section": section, "dom": dom}

    def rows(c):
        return pl.ds(c * block, block)

    def cols(ch):
        return pl.ds(starts[ch] * LANES, sizes[ch] * LANES)

    def span(chunks):
        return pl.ds(starts[chunks[0]] * LANES, sum(sizes[ch] for ch in chunks) * LANES)

    def own(slot, ch):
        return src.at[slot, rows(0), cols(ch)]

    def made_slot(c):
        return slabs + c

    def hist_slot(j):
        return 2 * slabs - 1 + j

    def lane(slot):
        return 1 if slot == 2 * slabs - 1 else slot

    e_copy = pltpu.make_async_copy(edges_hbm, edges, wsem.at[2])
    w_self = pltpu.make_async_copy(ws_hbm, ws, wsem.at[0])
    w_neigh = pltpu.make_async_copy(wn_hbm, wn, wsem.at[1])

    def given(j, slot):
        return pltpu.make_async_copy(stacked.at[rows(j)], src.at[slot, rows(0)], insem.at[j])

    @pl.when(is_first)
    def _():
        for j in range(slabs):
            given(j, j).start()

    @pl.when(s > 0)
    def _():
        for j in range(1, slabs):
            given(j, hist_slot(j)).start()

    barrier = pltpu.get_barrier_semaphore()

    def greet(section, dom):
        pl.semaphore_signal(barrier, inc=1, device_id=at(section, dom), device_id_type=MESH)

    for dom in (ahead, behind, across, partner):
        greet(s, dom)

    @pl.when(is_first)
    def _():
        for v in VIA:
            for dom in (ahead, across):
                greet(v, dom)

    for v in VIA:
        @pl.when(s == v)
        def _():
            greet(0, p)

    @pl.when(is_mid & (s > 1))
    def _():
        greet(s - 1, p)

    @pl.when(is_helper)
    def _():
        greet(top, p)
        greet(under, p)

    @pl.when(is_top)
    def _():
        greet(under, p)
        for dom in (p, ahead, across):
            greet(helper, dom)

    e_copy.start()
    w_self.start()
    w_neigh.start()

    def remote(src_ref, dst_ref, recv, section, dom, send=0):
        return pltpu.make_async_remote_copy(
            src_ref=src_ref, dst_ref=dst_ref, send_sem=gone.at[send], recv_sem=recv,
            device_id=at(section, dom), device_id_type=MESH,
        )

    def landed(ref, sem):
        pltpu.make_async_copy(ref, ref, sem).wait()

    def drain(units, send=0):
        if units:
            landed(ws.at[pl.ds(0, units * block * LANES // width)], gone.at[send])

    def start(copy):
        copy.start()

    def peer(src_ref, slot, ch, k, section, send):
        dom = behind if k == FAR else across
        return remote(
            src_ref, src.at[slot, rows(k + 1), cols(ch)],
            zrecv.at[lane(slot), ch, 0 if k == FAR else 1], section, dom, send,
        )

    def spread(src_ref, slot, ch, section, twice, send=0):
        start(peer(src_ref, slot, ch, FAR, section, send))

        @pl.when(is_odd)
        def _():
            start(peer(src_ref, slot, ch, BELOW, section, send))

        if ch in twice:
            @pl.when(is_even)
            def _():
                start(peer(src_ref, slot, ch, NEXT, section, send))

    def share(slot, ch):
        start(remote(
            own(slot, ch), src.at[slot, pl.ds((odd + 1) * block, block), cols(ch)],
            zrecv.at[lane(slot), ch, 1], s, partner,
        ))

    def exchange(slot, ch, twice):
        spread(own(slot, ch), slot, ch, s, twice)
        share(slot, ch)

    def relay(slot, ch, twice):
        ref = src.at[slot, rows(FAR + 1), cols(ch)]
        landed(ref, zrecv.at[lane(slot), ch, 0])
        if ch not in twice:
            @pl.when(is_even)
            def _():
                start(remote(
                    ref, src.at[slot, rows(NEXT + 1), cols(ch)], zrecv.at[lane(slot), ch, 1], s, partner,
                ))

    def rest(slot, ch):
        landed(src.at[slot, pl.ds(block, 2 * block), cols(ch)], zrecv.at[lane(slot), ch, 1])

    def hist_send(j):
        slot = hist_slot(j)
        mine = src.at[slot, rows(0)]
        start(remote(mine, src.at[slot, rows(FAR + 1)], hrecv.at[j - 1, 0], s, behind))

        @pl.when(is_odd)
        def _():
            start(remote(mine, src.at[slot, rows(BELOW + 1)], hrecv.at[j - 1, 1], s, across))

        start(remote(
            mine, src.at[slot, pl.ds((odd + 1) * block, block)], hrecv.at[j - 1, 1], s, partner,
        ))

    def hist_take(j):
        slot = hist_slot(j)
        ref = src.at[slot, rows(FAR + 1)]
        landed(ref, hrecv.at[j - 1, 0])

        @pl.when(is_even)
        def _():
            start(remote(ref, src.at[slot, rows(NEXT + 1)], hrecv.at[j - 1, 1], s, partner))

        landed(src.at[slot, pl.ds(block, 2 * block)], hrecv.at[j - 1, 1])

    def upward(src_ref, dst_ref, recv):
        start(remote(src_ref, dst_ref, recv, s + 1, p))

        @pl.when(s == under)
        def _():
            start(remote(src_ref, dst_ref, recv, s + 2, p, 1))

    def up(c, ch):
        part = stage.at[rows(c), cols(ch)]
        if c == 0:
            upward(part, own(0, ch), xrecv.at[ch])
        else:
            upward(part, above.at[c - 1, :, cols(ch)], arecv.at[c - 1])

    def sum_up(c, ch):
        upward(sums.at[c - 1, :, cols(ch)], below.at[c - 1, :, cols(ch)], srecv.at[c - 1, ch])

    def hand_back(c):
        return remote(
            src.at[made_slot(c), rows(0), pl.ds(0, half)], out.at[rows(c), pl.ds(0, half)],
            orecv.at[c], helper, p,
        )

    depth = width // QUARTERS
    bit = depth // PIECES
    pieces = [(m, h) for m in range(2) for h in range(PIECES)]

    def part(pair, m, owner, h):
        return pair[m].at[pl.ds(owner * depth + h * bit, bit), pl.ds(0, half)]

    def weight_up(m, h):
        start(remote(
            part((ws_hbm, wn_hbm), m, quarter, h), part((vs, vn), m, quarter, h),
            vrecv.at[0, m, h], top, p, 1,
        ))

    def weight_pass(m, h, dom, sem, owner, send=1):
        ref = part((vs, vn), m, owner, h)
        start(remote(ref, ref, sem, s, dom, send))

    @pl.when(is_first)
    def _():
        for j in range(slabs):
            given(j, j).wait()

    @pl.when(s > 0)
    def _():
        for j in range(1, slabs):
            given(j, hist_slot(j)).wait()

    def one(flag, amount=1):
        return jnp.where(flag, amount, 0)

    greetings = 4 + one(is_first, len(VIA)) + one(is_mid) + one(s == under) + one(is_helper, 3) + one(is_top)
    for v in VIA:
        greetings = greetings + one(s == v, 2)
    pl.semaphore_wait(barrier, greetings)

    def twice_given(j):
        return [ch for ch in how["twice_given"] if (j, ch) in detour]

    @pl.when(is_first)
    def _():
        for (j, ch), v in detour.items():
            start(remote(own(j, ch), alt.at[j, :, cols(ch)], trecv.at[j], v, p))
        for ch in everywhere:
            for j in range(slabs):
                if (j, ch) not in detour:
                    spread(own(j, ch), j, ch, s, twice_given(j))
                share(j, ch)

    @pl.when(is_helper)
    def _():
        for m, h in pieces:
            weight_up(m, h)

    for v in VIA:
        @pl.when(s == v)
        def _():
            for (j, ch), via in detour.items():
                if via == v:
                    ref = alt.at[j, :, cols(ch)]
                    landed(ref, trecv.at[j])
                    spread(ref, j, ch, 0, twice_given(j), 2)

    @pl.when(s > 0)
    def _():
        for j in range(1, slabs):
            hist_send(j)

    e_copy.wait()
    tile = lax.broadcasted_iota(jnp.int32, (block, edges.shape[1]), 1) // block
    degree = []
    for c in range(slabs):
        entries = edges[rows(c), :].astype(jnp.float32)
        total = jnp.ones((block, 1), jnp.float32)
        for j in range(slabs):
            scale = jnp.full(entries.shape, 1.0 if c == j else 0.0, jnp.float32)
            for k in range(len(PEER_OFFSETS)):
                wanted = jnp.where(picks[c, k] == j, 1.0, 0.0)
                scale = jnp.where(tile == k + 1, wanted, scale)
            masked = entries * scale
            masks[j, rows(c)] = masked.astype(jnp.bfloat16)
            total = total + jnp.sum(masked, axis=1, keepdims=True)
        degree.append(total)

    degrees = jnp.concatenate(degree, axis=0)

    def gather(j, slot, ch, dest=slice(None)):
        return jnp.dot(masks[j, dest], src[slot, :, cols(ch)], preferred_element_type=jnp.float32)

    def gathers(pairs, ch, dest=slice(None)):
        total = None
        for j, slot in pairs:
            term = gather(j, slot, ch, dest)
            total = term if total is None else total + term
        return total

    def own_rows(slots):
        return jnp.concatenate([src[slot, rows(0), :] for slot in slots], axis=0)

    def self_part(c, ref, weights, chunks=everywhere):
        acc[rows(c), span(chunks)] = jnp.dot(
            ref[...], weights[:, span(chunks)], preferred_element_type=jnp.float32
        )

    def finish_all(ch, summed, weights, emit, at_end):
        mean = (summed / degrees).astype(jnp.bfloat16)
        if not at_end:
            acc[...] += jnp.dot(mean, weights[cols(ch), :], preferred_element_type=jnp.float32)
            return
        for c in range(slabs):
            for n in everywhere:
                hidden = acc[rows(c), cols(n)] + jnp.dot(
                    mean[c * block:(c + 1) * block], weights[cols(ch), cols(n)],
                    preferred_element_type=jnp.float32,
                )
                emit(c, n, jnp.maximum(hidden, 0.0).astype(jnp.bfloat16))

    def finish(c, ch, summed, weights, emit, at_end, chunks=everywhere):
        mean = (summed / degree[c]).astype(jnp.bfloat16)
        if not at_end:
            acc[rows(c), span(chunks)] += jnp.dot(
                mean, weights[cols(ch), span(chunks)], preferred_element_type=jnp.float32
            )
            return
        for n in chunks:
            hidden = acc[rows(c), cols(n)] + jnp.dot(
                mean, weights[cols(ch), cols(n)], preferred_element_type=jnp.float32
            )
            emit(c, n, jnp.maximum(hidden, 0.0).astype(jnp.bfloat16))

    def put(c, chunks):
        start(pltpu.make_async_copy(
            stage.at[rows(c), span(chunks)], out.at[rows(c), span(chunks)], outsem.at[0]
        ))

    def emit_up(c, n, made):
        stage[rows(c), cols(n)] = made
        if c > 0:
            src[c + last, rows(0), cols(n)] = made
            exchange(c + last, n, how["twice"])
        up(c, n)
        if n == everywhere[-1]:
            put(c, everywhere)

    def emit_inner(c, n, made):
        src[made_slot(c), rows(0), cols(n)] = made
        exchange(made_slot(c), n, ())
        if n == near[-1]:
            start(hand_back(c))

    def emit_across(c, n, made):
        stage[rows(c), cols(n)] = made
        part = stage.at[rows(c), cols(n)]
        start(remote(part, own(made_slot(c), n), brecv.at[c, distant.index(n)], top, p))
        spread(part, made_slot(c), n, top, ())
        if n == distant[-1]:
            put(c, distant)

    def emit_out(c, n, made):
        stage[rows(c), cols(n)] = made
        put(c, [n])

    def in_turn(order, ready, use):
        ready(order[0])
        for i, ch in enumerate(order):
            if i + 1 < len(order):
                ready(order[i + 1])
            use(ch, i == len(order) - 1)

    def send_sums(c):
        def ready(ch):
            relay(c + last, ch, how["twice"])

        def use(ch, at_end):
            rest(c + last, ch)
            total = gathers([(j, j + last) for j in range(1, c + 1)], ch, rows(c))
            sums[c - 1, :, cols(ch)] = total.astype(jnp.bfloat16)
            sum_up(c, ch)

        in_turn(everywhere, ready, use)

    @pl.when(is_first)
    def _():
        w_self.wait()
        acc[...] = jnp.dot(own_rows(range(slabs)), ws[...], preferred_element_type=jnp.float32)
        w_neigh.wait()

        def ready(ch):
            for j in range(slabs):
                relay(j, ch, twice_given(j))

        def use(ch, at_end):
            for j in range(slabs):
                rest(j, ch)
            finish_all(ch, gathers([(j, j) for j in range(slabs)], ch), wn, emit_up, at_end)

        in_turn(how["given"], ready, use)
        for c in range(1, slabs):
            send_sums(c)

    def first_slab_up():
        for ch in everywhere:
            landed(own(0, ch), xrecv.at[ch])
            exchange(0, ch, how["twice"])

    def layer_above(w_s, w_n, emit, after, chunks=everywhere, weights_in=lambda: None):
        first_slab_up()
        weights_in()
        self_part(0, src.at[0, rows(0)], w_s, chunks)

        def ready(ch):
            relay(0, ch, how["twice"])

        def use(ch, at_end):
            if ch == everywhere[how["early"]]:
                for c in range(1, slabs):
                    landed(above.at[c - 1], arecv.at[c - 1])
                    self_part(c, above.at[c - 1], w_s, chunks)
            rest(0, ch)
            total = pre[:, cols(ch)] + gather(0, 0, ch)
            pre[:, cols(ch)] = total
            finish(0, ch, total[:block], w_n, emit, at_end, chunks)

        in_turn(everywhere, ready, use)
        for c in range(1, slabs):
            for ch in everywhere:
                landed(below.at[c - 1, :, cols(ch)], srecv.at[c - 1, ch])
                finish(
                    c, ch, pre[rows(c), cols(ch)] + below[c - 1, :, cols(ch)].astype(jnp.float32),
                    w_n, emit, ch == everywhere[-1], chunks,
                )
            after(c)

    def hist_sums():
        for c in range(last):
            pre[rows(c)] = jnp.dot(
                masks[c + 1, rows(c)], src[hist_slot(c + 1)], preferred_element_type=jnp.float32
            )
            for j in range(c + 2, slabs):
                pre[rows(c)] += jnp.dot(
                    masks[j, rows(c)], src[hist_slot(j)], preferred_element_type=jnp.float32
                )
        pre[rows(last)] = jnp.zeros((block, width), jnp.float32)

    @pl.when(is_mid)
    def _():
        for j in range(1, slabs):
            hist_take(j)
        hist_sums()
        w_self.wait()
        w_neigh.wait()
        layer_above(ws, wn, emit_up, send_sums)

    @pl.when(is_helper)
    def _():
        for j in range(1, slabs):
            hist_take(j)
        hist_sums()
        for c in range(last):
            sums[c] = pre[rows(c)].astype(jnp.bfloat16)
            start(remote(sums.at[c], histsum.at[c], qrecv.at[c], top, p))
        w_self.wait()
        w_neigh.wait()
        layer_above(ws, wn, emit_across, lambda c: None, distant)

    @pl.when(is_top)
    def _():
        for m, h in pieces:
            landed(part((vs, vn), m, 0, h), vrecv.at[0, m, h])
            weight_pass(m, h, partner, precv.at[0], quarter)
            weight_pass(m, h, twin, vrecv.at[1, m, h], quarter, 2)
        for j in range(1, slabs):
            hist_take(j)
        for m, h in pieces:
            landed(part((vs, vn), m, 0, h), vrecv.at[1, m, h])
            weight_pass(m, h, partner, precv.at[1], lax.rem(quarter + 2, QUARTERS))
        everything = 2 * depth * half // (block * LANES)

        def weights_in():
            for i in range(2):
                landed(vs.at[pl.ds(0, 2 * depth), pl.ds(0, half)], precv.at[i])

        for c in range(slabs):
            if c < last:
                landed(histsum.at[c], qrecv.at[c])
                pre[rows(c)] = histsum[c].astype(jnp.float32)
            else:
                pre[rows(c)] = jnp.zeros((block, width), jnp.float32)
        w_self.wait()
        w_neigh.wait()
        layer_above(vs, vn, emit_inner, lambda c: None, near, weights_in)
        drain(2 * everything, 1)
        drain(everything, 2)
        hist_sums()
        slots = [made_slot(c) for c in range(slabs)]

        def given_up(c):
            for ch in distant:
                landed(own(slots[c], ch), brecv.at[c, distant.index(ch)])
                share(slots[c], ch)

        def relays(c, chunks):
            for ch in chunks:
                relay(slots[c], ch, ())

        def use(ch, at_end=False):
            for c in range(slabs):
                rest(slots[c], ch)
            total = pre[:, cols(ch)]
            for c in range(slabs):
                term = gather(c, slots[c], ch, pl.ds(c * block, (slabs - c) * block))
                if c > 0:
                    term = jnp.concatenate([jnp.zeros((c * block, term.shape[1]), jnp.float32), term], axis=0)
                total = total + term
            finish_all(ch, total, wn, emit_out, at_end)

        def own_part(chunks):
            mine = jnp.concatenate([src[slot, rows(0), span(chunks)] for slot in slots], axis=0)
            return jnp.dot(mine, ws[span(chunks), :], preferred_element_type=jnp.float32)

        acc[...] = own_part(near)
        for c in range(slabs):
            relays(c, near)
        for c in range(slabs):
            given_up(c)
            relays(c, distant)
        acc[...] += own_part(distant)
        for ch in everywhere:
            use(ch, ch == everywhere[-1])

    full = sum(sizes)
    part_units = sum(sizes[ch] for ch in distant)

    def by_parity(even, odd_units):
        @pl.when(is_even)
        def _():
            drain(even)

        @pl.when(is_odd)
        def _():
            drain(odd_units)

    @pl.when(jnp.logical_not(is_helper))
    def _():
        landed(stage, outsem.at[0])

    for v in VIA:
        @pl.when(s == v)
        def _():
            count = [sum(sizes[ch] for (j, ch), via in detour.items() if via == v), 0]
            count[1] = sum(
                sizes[ch] for (j, ch), via in detour.items() if via == v and ch in twice_given(j)
            )

            @pl.when(is_odd)
            def _():
                drain(2 * count[0], 2)

            @pl.when(is_even)
            def _():
                drain(count[0] + count[1], 2)

    @pl.when(is_first)
    def _():
        detoured = sum(sizes[ch] for _, ch in detour)
        twice_units = sum(sizes[ch] for j, ch in detour if ch in twice_given(j))
        base = 3 * full * slabs + full * slabs + last * 4 * full
        by_parity(base - twice_units, base - detoured)

    @pl.when(is_mid)
    def _():
        drain(3 * full * slabs + full * slabs + last * 4 * full)

    @pl.when(s == under)
    def _():
        @pl.when(sends_up)
        def _():
            drain(full * slabs + last * full, 1)

    @pl.when(is_helper)
    def _():
        landed(stage.at[:, span(distant)], outsem.at[0])
        drain(2 * depth * half // (block * LANES), 1)
        base = 3 * full * slabs + last * full + 2 * part_units * slabs
        by_parity(base, base + part_units * slabs)
        for c in range(slabs):
            hand_back(c).wait_recv()

    @pl.when(is_top)
    def _():
        near_units = full - part_units
        base = 3 * full * slabs + 4 * near_units * slabs + part_units * slabs
        by_parity(base + part_units * slabs, base)


def per_device(ns, nd, stacked, edges, picks, self_w, neigh_w):
    _, node_rows, width = stacked.shape
    tiles = len(PEER_OFFSETS) + 1
    block = edges.shape[1] // tiles
    slabs = node_rows // block
    slots = 3 * slabs - 1
    others = max(1, slabs - 1)
    how = plan(width)
    nch = len(how["sizes"])
    half = sum(how["sizes"][ch] for ch in how["near"]) * LANES
    anywhere = pl.BlockSpec(memory_space=pl.ANY)
    bf16, f32 = jnp.bfloat16, jnp.float32
    sem = pltpu.SemaphoreType.DMA
    result = pl.pallas_call(
        functools.partial(kernel, ns, nd, slabs),
        out_shape=jax.ShapeDtypeStruct((node_rows, width), bf16),
        in_specs=[anywhere, anywhere, pl.BlockSpec(memory_space=pltpu.SMEM), anywhere, anywhere],
        out_specs=anywhere,
        scratch_shapes=[
            pltpu.VMEM((width, width), bf16),
            pltpu.VMEM((width, width), bf16),
            pltpu.VMEM((width, half), bf16),
            pltpu.VMEM((width, half), bf16),
            pltpu.VMEM(edges.shape, jnp.int32),
            pltpu.VMEM((slots, tiles * block, width), bf16),
            pltpu.VMEM((slabs, block, width), bf16),
            pltpu.VMEM((slabs, slabs * block, tiles * block), bf16),
            pltpu.VMEM((slabs * block, width), f32),
            pltpu.VMEM((slabs * block, width), f32),
            pltpu.VMEM((slabs * block, width), bf16),
            pltpu.VMEM((others, block, width), bf16),
            pltpu.VMEM((slabs, block, width), bf16),
            pltpu.VMEM((others, block, width), bf16),
            pltpu.VMEM((others, block, width), bf16),
            sem((3,)),
            sem((slabs,)),
            sem((1,)),
            sem((3,)),
            sem((max(2, 2 * slabs - 1), nch, 2)),
            sem((others, 2)),
            sem((nch,)),
            sem((others,)),
            sem((others, nch)),
            sem((slabs, len(how["distant"]))),
            sem((slabs,)),
            sem((others,)),
            sem((slabs,)),
            sem((2, 2, PIECES)),
            sem((2,)),
        ],
        compiler_params=pltpu.CompilerParams(collective_id=0, has_side_effects=True),
    )(stacked[0], edges, picks, self_w[0], neigh_w[0])
    return result[None]


def solution(mesh):
    in_specs = (
        P("section", "dom", None),
        P("dom", None),
        P("dom", None),
        P("section", None, None),
        P("section", None, None),
    )
    out_specs = P("section", "dom", None)
    ns, nd = mesh.shape["section"], mesh.shape["dom"]
    return jax.shard_map(
        functools.partial(per_device, ns, nd),
        mesh=mesh, in_specs=in_specs, out_specs=out_specs, check_vma=False,
    )
```

```python
import functools

import jax
import jax.numpy as jnp
from jax import lax
from jax.experimental import pallas as pl
from jax.experimental.pallas import tpu as pltpu
from jax.sharding import PartitionSpec as P

PEER_OFFSETS = (-1, 1, 2)
MESH = pl.DeviceIdType.MESH
BELOW, NEXT, FAR = range(3)
LANES = 128
QUARTERS, PIECES = 4, 2
VIA = (1, 2)


def plan(width):
    units = width // LANES
    near = units * 5 // 8
    far = units - near
    sizes = [near * 2 // 5, near - near * 2 // 5, far - far // 3, far // 3]
    starts = [sum(sizes[:i]) for i in range(len(sizes))]
    return {
        "sizes": sizes,
        "starts": starts,
        "near": [0, 1],
        "distant": [2, 3],
        "detour": {(0, 2): VIA[0], (1, 2): VIA[1]},
        "given": [0, 1, 3, 2],
        "twice": {3},
        "early": 1,
        "twice_given": {2},
    }


def kernel(
    ns, nd, slabs,
    stacked, edges_hbm, picks, ws_hbm, wn_hbm, out,
    ws, wn, vs, vn, edges, src, alt, masks, pre, acc, stage, above, sums, below, histsum,
    wsem, insem, outsem, gone, zrecv, hrecv, xrecv, arecv, srecv, brecv, trecv, qrecv, orecv,
    vrecv, precv,
):
    tiles = len(PEER_OFFSETS) + 1
    block = edges.shape[1] // tiles
    width = stacked.shape[1]
    how = plan(width)
    sizes, starts, near, distant = (how[key] for key in ("sizes", "starts", "near", "distant"))
    detour = {unit: via for unit, via in how["detour"].items() if unit[0] < slabs}
    everywhere = list(range(len(sizes)))
    half = sum(sizes[ch] for ch in near) * LANES
    last = slabs - 1
    s = lax.axis_index("section")
    p = lax.axis_index("dom")
    odd = lax.rem(p, 2)
    is_odd, is_even = odd == 1, odd == 0
    partner = p + 1 - 2 * odd
    across = lax.rem(p - 1 + 2 * odd + nd, nd)
    ahead, behind = lax.rem(p + 2, nd), lax.rem(p + nd - 2, nd)
    quarter = lax.rem(p, QUARTERS)
    twin = jnp.where(quarter < 2, p + 2, p - 2)
    top, helper, under = ns - 1, ns - 2, ns - 3
    is_first, is_top, is_helper = s == 0, s == top, s == helper
    is_mid = (s > 0) & (s <= under)
    sends_up = s <= under

    def at(section, dom):
        return {"section": section, "dom": dom}

    def rows(c):
        return pl.ds(c * block, block)

    def cols(ch):
        return pl.ds(starts[ch] * LANES, sizes[ch] * LANES)

    def span(chunks):
        return pl.ds(starts[chunks[0]] * LANES, sum(sizes[ch] for ch in chunks) * LANES)

    def own(slot, ch):
        return src.at[slot, rows(0), cols(ch)]

    def made_slot(c):
        return slabs + c

    def hist_slot(j):
        return 2 * slabs - 1 + j

    def lane(slot):
        return 1 if slot == 2 * slabs - 1 else slot

    e_copy = pltpu.make_async_copy(edges_hbm, edges, wsem.at[2])
    w_self = pltpu.make_async_copy(ws_hbm, ws, wsem.at[0])
    w_neigh = pltpu.make_async_copy(wn_hbm, wn, wsem.at[1])

    def given(j, slot):
        return pltpu.make_async_copy(stacked.at[rows(j)], src.at[slot, rows(0)], insem.at[j])

    @pl.when(is_first)
    def _():
        for j in range(slabs):
            given(j, j).start()

    @pl.when(s > 0)
    def _():
        for j in range(1, slabs):
            given(j, hist_slot(j)).start()

    barrier = pltpu.get_barrier_semaphore()

    def greet(section, dom):
        pl.semaphore_signal(barrier, inc=1, device_id=at(section, dom), device_id_type=MESH)

    for dom in (ahead, behind, across, partner):
        greet(s, dom)

    @pl.when(is_first)
    def _():
        for v in VIA:
            for dom in (ahead, across):
                greet(v, dom)

    for v in VIA:
        @pl.when(s == v)
        def _():
            greet(0, p)

    @pl.when(is_mid & (s > 1))
    def _():
        greet(s - 1, p)

    @pl.when(is_helper)
    def _():
        greet(top, p)
        greet(under, p)

    @pl.when(is_top)
    def _():
        greet(under, p)
        for dom in (p, ahead, across):
            greet(helper, dom)

    e_copy.start()
    w_self.start()
    w_neigh.start()

    def remote(src_ref, dst_ref, recv, section, dom, send=0):
        return pltpu.make_async_remote_copy(
            src_ref=src_ref, dst_ref=dst_ref, send_sem=gone.at[send], recv_sem=recv,
            device_id=at(section, dom), device_id_type=MESH,
        )

    def landed(ref, sem):
        pltpu.make_async_copy(ref, ref, sem).wait()

    def drain(units, send=0):
        if units:
            landed(ws.at[pl.ds(0, units * block * LANES // width)], gone.at[send])

    def start(copy):
        copy.start()

    def peer(src_ref, slot, ch, k, section, send):
        dom = behind if k == FAR else across
        return remote(
            src_ref, src.at[slot, rows(k + 1), cols(ch)],
            zrecv.at[lane(slot), ch, 0 if k == FAR else 1], section, dom, send,
        )

    def spread(src_ref, slot, ch, section, twice, send=0):
        start(peer(src_ref, slot, ch, FAR, section, send))

        @pl.when(is_odd)
        def _():
            start(peer(src_ref, slot, ch, BELOW, section, send))

        if ch in twice:
            @pl.when(is_even)
            def _():
                start(peer(src_ref, slot, ch, NEXT, section, send))

    def share(slot, ch):
        start(remote(
            own(slot, ch), src.at[slot, pl.ds((odd + 1) * block, block), cols(ch)],
            zrecv.at[lane(slot), ch, 1], s, partner,
        ))

    def exchange(slot, ch, twice):
        spread(own(slot, ch), slot, ch, s, twice)
        share(slot, ch)

    def relay(slot, ch, twice):
        ref = src.at[slot, rows(FAR + 1), cols(ch)]
        landed(ref, zrecv.at[lane(slot), ch, 0])
        if ch not in twice:
            @pl.when(is_even)
            def _():
                start(remote(
                    ref, src.at[slot, rows(NEXT + 1), cols(ch)], zrecv.at[lane(slot), ch, 1], s, partner,
                ))

    def rest(slot, ch):
        landed(src.at[slot, pl.ds(block, 2 * block), cols(ch)], zrecv.at[lane(slot), ch, 1])

    def hist_send(j):
        slot = hist_slot(j)
        mine = src.at[slot, rows(0)]
        start(remote(mine, src.at[slot, rows(FAR + 1)], hrecv.at[j - 1, 0], s, behind))

        @pl.when(is_odd)
        def _():
            start(remote(mine, src.at[slot, rows(BELOW + 1)], hrecv.at[j - 1, 1], s, across))

        start(remote(
            mine, src.at[slot, pl.ds((odd + 1) * block, block)], hrecv.at[j - 1, 1], s, partner,
        ))

    def hist_take(j):
        slot = hist_slot(j)
        ref = src.at[slot, rows(FAR + 1)]
        landed(ref, hrecv.at[j - 1, 0])

        @pl.when(is_even)
        def _():
            start(remote(ref, src.at[slot, rows(NEXT + 1)], hrecv.at[j - 1, 1], s, partner))

        landed(src.at[slot, pl.ds(block, 2 * block)], hrecv.at[j - 1, 1])

    def upward(src_ref, dst_ref, recv):
        start(remote(src_ref, dst_ref, recv, s + 1, p))

        @pl.when(s == under)
        def _():
            start(remote(src_ref, dst_ref, recv, s + 2, p, 1))

    def up(c, ch):
        part = stage.at[rows(c), cols(ch)]
        if c == 0:
            upward(part, own(0, ch), xrecv.at[ch])
        else:
            upward(part, above.at[c - 1, :, cols(ch)], arecv.at[c - 1])

    def sum_up(c, ch):
        upward(sums.at[c - 1, :, cols(ch)], below.at[c - 1, :, cols(ch)], srecv.at[c - 1, ch])

    def hand_back(c):
        return remote(
            src.at[made_slot(c), rows(0), pl.ds(0, half)], out.at[rows(c), pl.ds(0, half)],
            orecv.at[c], helper, p,
        )

    depth = width // QUARTERS
    bit = depth // PIECES
    pieces = [(m, h) for m in range(2) for h in range(PIECES)]

    def part(pair, m, owner, h):
        return pair[m].at[pl.ds(owner * depth + h * bit, bit), pl.ds(0, half)]

    def weight_up(m, h):
        start(remote(
            part((ws_hbm, wn_hbm), m, quarter, h), part((vs, vn), m, quarter, h),
            vrecv.at[0, m, h], top, p, 1,
        ))

    def weight_pass(m, h, dom, sem, owner, send=1):
        ref = part((vs, vn), m, owner, h)
        start(remote(ref, ref, sem, s, dom, send))

    @pl.when(is_first)
    def _():
        for j in range(slabs):
            given(j, j).wait()

    @pl.when(s > 0)
    def _():
        for j in range(1, slabs):
            given(j, hist_slot(j)).wait()

    def one(flag, amount=1):
        return jnp.where(flag, amount, 0)

    greetings = 4 + one(is_first, len(VIA)) + one(is_mid) + one(s == under) + one(is_helper, 3) + one(is_top)
    for v in VIA:
        greetings = greetings + one(s == v, 2)
    pl.semaphore_wait(barrier, greetings)

    def twice_given(j):
        return [ch for ch in how["twice_given"] if (j, ch) in detour]

    @pl.when(is_first)
    def _():
        for (j, ch), v in detour.items():
            start(remote(own(j, ch), alt.at[j, :, cols(ch)], trecv.at[j], v, p))
        for ch in everywhere:
            for j in range(slabs):
                if (j, ch) not in detour:
                    spread(own(j, ch), j, ch, s, twice_given(j))
                share(j, ch)

    @pl.when(is_helper)
    def _():
        for m, h in pieces:
            weight_up(m, h)

    for v in VIA:
        @pl.when(s == v)
        def _():
            for (j, ch), via in detour.items():
                if via == v:
                    ref = alt.at[j, :, cols(ch)]
                    landed(ref, trecv.at[j])
                    spread(ref, j, ch, 0, twice_given(j), 2)

    @pl.when(s > 0)
    def _():
        for j in range(1, slabs):
            hist_send(j)

    e_copy.wait()
    tile = lax.broadcasted_iota(jnp.int32, (block, edges.shape[1]), 1) // block
    degree = []
    for c in range(slabs):
        entries = edges[rows(c), :].astype(jnp.float32)
        total = jnp.ones((block, 1), jnp.float32)
        for j in range(slabs):
            scale = jnp.full(entries.shape, 1.0 if c == j else 0.0, jnp.float32)
            for k in range(len(PEER_OFFSETS)):
                wanted = jnp.where(picks[c, k] == j, 1.0, 0.0)
                scale = jnp.where(tile == k + 1, wanted, scale)
            masked = entries * scale
            masks[j, rows(c)] = masked.astype(jnp.bfloat16)
            total = total + jnp.sum(masked, axis=1, keepdims=True)
        degree.append(total)

    degrees = jnp.concatenate(degree, axis=0)

    def gather(j, slot, ch, dest=slice(None)):
        return jnp.dot(masks[j, dest], src[slot, :, cols(ch)], preferred_element_type=jnp.float32)

    def gathers(pairs, ch, dest=slice(None)):
        total = None
        for j, slot in pairs:
            term = gather(j, slot, ch, dest)
            total = term if total is None else total + term
        return total

    def own_rows(slots):
        return jnp.concatenate([src[slot, rows(0), :] for slot in slots], axis=0)

    def self_part(c, ref, weights, chunks=everywhere):
        acc[rows(c), span(chunks)] = jnp.dot(
            ref[...], weights[:, span(chunks)], preferred_element_type=jnp.float32
        )

    def finish_all(ch, summed, weights, emit, at_end):
        mean = (summed / degrees).astype(jnp.bfloat16)
        if not at_end:
            acc[...] += jnp.dot(mean, weights[cols(ch), :], preferred_element_type=jnp.float32)
            return
        for c in range(slabs):
            for n in everywhere:
                hidden = acc[rows(c), cols(n)] + jnp.dot(
                    mean[c * block:(c + 1) * block], weights[cols(ch), cols(n)],
                    preferred_element_type=jnp.float32,
                )
                emit(c, n, jnp.maximum(hidden, 0.0).astype(jnp.bfloat16))

    def finish(c, ch, summed, weights, emit, at_end, chunks=everywhere):
        mean = (summed / degree[c]).astype(jnp.bfloat16)
        if not at_end:
            acc[rows(c), span(chunks)] += jnp.dot(
                mean, weights[cols(ch), span(chunks)], preferred_element_type=jnp.float32
            )
            return
        for n in chunks:
            hidden = acc[rows(c), cols(n)] + jnp.dot(
                mean, weights[cols(ch), cols(n)], preferred_element_type=jnp.float32
            )
            emit(c, n, jnp.maximum(hidden, 0.0).astype(jnp.bfloat16))

    def put(c, chunks):
        start(pltpu.make_async_copy(
            stage.at[rows(c), span(chunks)], out.at[rows(c), span(chunks)], outsem.at[0]
        ))

    def emit_up(c, n, made):
        stage[rows(c), cols(n)] = made
        if c > 0:
            src[c + last, rows(0), cols(n)] = made
            exchange(c + last, n, how["twice"])
        up(c, n)
        if n == everywhere[-1]:
            put(c, everywhere)

    def emit_inner(c, n, made):
        src[made_slot(c), rows(0), cols(n)] = made
        exchange(made_slot(c), n, ())
        if n == near[-1]:
            start(hand_back(c))

    def emit_across(c, n, made):
        stage[rows(c), cols(n)] = made
        part = stage.at[rows(c), cols(n)]
        start(remote(part, own(made_slot(c), n), brecv.at[c, distant.index(n)], top, p))
        spread(part, made_slot(c), n, top, ())
        if n == distant[-1]:
            put(c, distant)

    def emit_out(c, n, made):
        stage[rows(c), cols(n)] = made
        put(c, [n])

    def in_turn(order, ready, use):
        ready(order[0])
        for i, ch in enumerate(order):
            if i + 1 < len(order):
                ready(order[i + 1])
            use(ch, i == len(order) - 1)

    def send_sums(c):
        def ready(ch):
            relay(c + last, ch, how["twice"])

        def use(ch, at_end):
            rest(c + last, ch)
            total = gathers([(j, j + last) for j in range(1, c + 1)], ch, rows(c))
            sums[c - 1, :, cols(ch)] = total.astype(jnp.bfloat16)
            sum_up(c, ch)

        in_turn(everywhere, ready, use)

    @pl.when(is_first)
    def _():
        w_self.wait()
        acc[...] = jnp.dot(own_rows(range(slabs)), ws[...], preferred_element_type=jnp.float32)
        w_neigh.wait()

        def ready(ch):
            for j in range(slabs):
                relay(j, ch, twice_given(j))

        def use(ch, at_end):
            for j in range(slabs):
                rest(j, ch)
            finish_all(ch, gathers([(j, j) for j in range(slabs)], ch), wn, emit_up, at_end)

        in_turn(how["given"], ready, use)
        for c in range(1, slabs):
            send_sums(c)

    def first_slab_up():
        for ch in everywhere:
            landed(own(0, ch), xrecv.at[ch])
            exchange(0, ch, how["twice"])

    def layer_above(w_s, w_n, emit, after, chunks=everywhere, weights_in=lambda: None):
        first_slab_up()
        weights_in()
        self_part(0, src.at[0, rows(0)], w_s, chunks)

        def ready(ch):
            relay(0, ch, how["twice"])

        def use(ch, at_end):
            if ch == everywhere[how["early"]]:
                for c in range(1, slabs):
                    landed(above.at[c - 1], arecv.at[c - 1])
                    self_part(c, above.at[c - 1], w_s, chunks)
            rest(0, ch)
            total = pre[:, cols(ch)] + gather(0, 0, ch)
            pre[:, cols(ch)] = total
            finish(0, ch, total[:block], w_n, emit, at_end, chunks)

        in_turn(everywhere, ready, use)
        for c in range(1, slabs):
            for ch in everywhere:
                landed(below.at[c - 1, :, cols(ch)], srecv.at[c - 1, ch])
                finish(
                    c, ch, pre[rows(c), cols(ch)] + below[c - 1, :, cols(ch)].astype(jnp.float32),
                    w_n, emit, ch == everywhere[-1], chunks,
                )
            after(c)

    def hist_sums():
        for c in range(last):
            pre[rows(c)] = jnp.dot(
                masks[c + 1, rows(c)], src[hist_slot(c + 1)], preferred_element_type=jnp.float32
            )
            for j in range(c + 2, slabs):
                pre[rows(c)] += jnp.dot(
                    masks[j, rows(c)], src[hist_slot(j)], preferred_element_type=jnp.float32
                )
        pre[rows(last)] = jnp.zeros((block, width), jnp.float32)

    @pl.when(is_mid)
    def _():
        for j in range(1, slabs):
            hist_take(j)
        hist_sums()
        w_self.wait()
        w_neigh.wait()
        layer_above(ws, wn, emit_up, send_sums)

    @pl.when(is_helper)
    def _():
        for j in range(1, slabs):
            hist_take(j)
        hist_sums()
        for c in range(last):
            sums[c] = pre[rows(c)].astype(jnp.bfloat16)
            start(remote(sums.at[c], histsum.at[c], qrecv.at[c], top, p))
        w_self.wait()
        w_neigh.wait()
        layer_above(ws, wn, emit_across, lambda c: None, distant)

    @pl.when(is_top)
    def _():
        for m, h in pieces:
            landed(part((vs, vn), m, 0, h), vrecv.at[0, m, h])
            weight_pass(m, h, partner, precv.at[0], quarter)
            weight_pass(m, h, twin, vrecv.at[1, m, h], quarter, 2)
        for j in range(1, slabs):
            hist_take(j)
        for m, h in pieces:
            landed(part((vs, vn), m, 0, h), vrecv.at[1, m, h])
            weight_pass(m, h, partner, precv.at[1], lax.rem(quarter + 2, QUARTERS))
        everything = 2 * depth * half // (block * LANES)

        def weights_in():
            for i in range(2):
                landed(vs.at[pl.ds(0, 2 * depth), pl.ds(0, half)], precv.at[i])

        for c in range(slabs):
            if c < last:
                landed(histsum.at[c], qrecv.at[c])
                pre[rows(c)] = histsum[c].astype(jnp.float32)
            else:
                pre[rows(c)] = jnp.zeros((block, width), jnp.float32)
        w_self.wait()
        w_neigh.wait()
        layer_above(vs, vn, emit_inner, lambda c: None, near, weights_in)
        drain(2 * everything, 1)
        drain(everything, 2)
        hist_sums()
        slots = [made_slot(c) for c in range(slabs)]

        def given_up(c):
            for ch in distant:
                landed(own(slots[c], ch), brecv.at[c, distant.index(ch)])
                share(slots[c], ch)

        def relays(c, chunks):
            for ch in chunks:
                relay(slots[c], ch, ())

        def use(ch, at_end=False):
            mine = [last] if ch in near else range(slabs)
            for c in mine:
                rest(slots[c], ch)
            total = pre[:, cols(ch)]
            for c in mine:
                term = gather(c, slots[c], ch, pl.ds(c * block, (slabs - c) * block))
                if c > 0:
                    term = jnp.concatenate([jnp.zeros((c * block, term.shape[1]), jnp.float32), term], axis=0)
                total = total + term
            finish_all(ch, total, wn, emit_out, at_end)

        def own_part(chunks):
            mine = jnp.concatenate([src[slot, rows(0), span(chunks)] for slot in slots], axis=0)
            return jnp.dot(mine, ws[span(chunks), :], preferred_element_type=jnp.float32)

        acc[...] = own_part(near)
        for c in range(slabs):
            relays(c, near)
        for c in range(slabs):
            if c == last:
                for ch in near:
                    for j in range(last):
                        rest(slots[j], ch)
                        pre[j * block:, cols(ch)] += gather(
                            j, slots[j], ch, pl.ds(j * block, (slabs - j) * block)
                        )
            given_up(c)
            relays(c, distant)
        acc[...] += own_part(distant)
        for ch in everywhere:
            use(ch, ch == everywhere[-1])

    full = sum(sizes)
    part_units = sum(sizes[ch] for ch in distant)

    def by_parity(even, odd_units):
        @pl.when(is_even)
        def _():
            drain(even)

        @pl.when(is_odd)
        def _():
            drain(odd_units)

    @pl.when(jnp.logical_not(is_helper))
    def _():
        landed(stage, outsem.at[0])

    for v in VIA:
        @pl.when(s == v)
        def _():
            count = [sum(sizes[ch] for (j, ch), via in detour.items() if via == v), 0]
            count[1] = sum(
                sizes[ch] for (j, ch), via in detour.items() if via == v and ch in twice_given(j)
            )

            @pl.when(is_odd)
            def _():
                drain(2 * count[0], 2)

            @pl.when(is_even)
            def _():
                drain(count[0] + count[1], 2)

    @pl.when(is_first)
    def _():
        detoured = sum(sizes[ch] for _, ch in detour)
        twice_units = sum(sizes[ch] for j, ch in detour if ch in twice_given(j))
        base = 3 * full * slabs + full * slabs + last * 4 * full
        by_parity(base - twice_units, base - detoured)

    @pl.when(is_mid)
    def _():
        drain(3 * full * slabs + full * slabs + last * 4 * full)

    @pl.when(s == under)
    def _():
        @pl.when(sends_up)
        def _():
            drain(full * slabs + last * full, 1)

    @pl.when(is_helper)
    def _():
        landed(stage.at[:, span(distant)], outsem.at[0])
        drain(2 * depth * half // (block * LANES), 1)
        base = 3 * full * slabs + last * full + 2 * part_units * slabs
        by_parity(base, base + part_units * slabs)
        for c in range(slabs):
            hand_back(c).wait_recv()

    @pl.when(is_top)
    def _():
        near_units = full - part_units
        base = 3 * full * slabs + 4 * near_units * slabs + part_units * slabs
        by_parity(base + part_units * slabs, base)


def per_device(ns, nd, stacked, edges, picks, self_w, neigh_w):
    _, node_rows, width = stacked.shape
    tiles = len(PEER_OFFSETS) + 1
    block = edges.shape[1] // tiles
    slabs = node_rows // block
    slots = 3 * slabs - 1
    others = max(1, slabs - 1)
    how = plan(width)
    nch = len(how["sizes"])
    half = sum(how["sizes"][ch] for ch in how["near"]) * LANES
    anywhere = pl.BlockSpec(memory_space=pl.ANY)
    bf16, f32 = jnp.bfloat16, jnp.float32
    sem = pltpu.SemaphoreType.DMA
    result = pl.pallas_call(
        functools.partial(kernel, ns, nd, slabs),
        out_shape=jax.ShapeDtypeStruct((node_rows, width), bf16),
        in_specs=[anywhere, anywhere, pl.BlockSpec(memory_space=pltpu.SMEM), anywhere, anywhere],
        out_specs=anywhere,
        scratch_shapes=[
            pltpu.VMEM((width, width), bf16),
            pltpu.VMEM((width, width), bf16),
            pltpu.VMEM((width, half), bf16),
            pltpu.VMEM((width, half), bf16),
            pltpu.VMEM(edges.shape, jnp.int32),
            pltpu.VMEM((slots, tiles * block, width), bf16),
            pltpu.VMEM((slabs, block, width), bf16),
            pltpu.VMEM((slabs, slabs * block, tiles * block), bf16),
            pltpu.VMEM((slabs * block, width), f32),
            pltpu.VMEM((slabs * block, width), f32),
            pltpu.VMEM((slabs * block, width), bf16),
            pltpu.VMEM((others, block, width), bf16),
            pltpu.VMEM((slabs, block, width), bf16),
            pltpu.VMEM((others, block, width), bf16),
            pltpu.VMEM((others, block, width), bf16),
            sem((3,)),
            sem((slabs,)),
            sem((1,)),
            sem((3,)),
            sem((max(2, 2 * slabs - 1), nch, 2)),
            sem((others, 2)),
            sem((nch,)),
            sem((others,)),
            sem((others, nch)),
            sem((slabs, len(how["distant"]))),
            sem((slabs,)),
            sem((others,)),
            sem((slabs,)),
            sem((2, 2, PIECES)),
            sem((2,)),
        ],
        compiler_params=pltpu.CompilerParams(collective_id=0, has_side_effects=True),
    )(stacked[0], edges, picks, self_w[0], neigh_w[0])
    return result[None]


def solution(mesh):
    in_specs = (
        P("section", "dom", None),
        P("dom", None),
        P("dom", None),
        P("section", None, None),
        P("section", None, None),
    )
    out_specs = P("section", "dom", None)
    ns, nd = mesh.shape["section"], mesh.shape["dom"]
    return jax.shard_map(
        functools.partial(per_device, ns, nd),
        mesh=mesh, in_specs=in_specs, out_specs=out_specs, check_vma=False,
    )
```
